32 devices in a mesh: date: 2 (over x), blk: 8 (over z, y), sect: 2 (over core).
Axes of the slice: x: 2, y: 2, z: 4, core: 2. Of those that a mesh axis runs over, the one named last changes fastest.
Arguments:
- obs_weight: bfloat16 [16, 2, 512, 128], P(('date', 'blk'), 'sect'), parts along dimension 0, may hold values from -4 to 4
- obs_frac: bfloat16 [16, 2, 2, 512], P(('date', 'blk'), 'sect'), parts along dimension 0, may hold values from 0 to 1
- obs_cell: int32 [16, 2, 512], P(('date', 'blk'), 'sect'), parts along dimension 0, may hold values from 0 to 127
- obs_level: int32 [16, 2, 512], P(('date', 'blk'), 'sect'), parts along dimension 0, may hold values from 0 to 63
- obs_count: int32 [16, 2], P(('date', 'blk'), 'sect'), parts along dimension 0, may hold values from 1 to 512, as said below
- reach: int32 [16, 2], P(('date', 'blk')), parts along dimension 0, may hold values from 0 to 3, as said below
- length_x: float32 [64], replicated, may hold values from 0.5 to 2
- length_y: float32 [64], replicated, may hold values from 0.1 to 0.5
- tilt: float32 [64], replicated, may hold values from -0.7 to 0.7
- vert_len: float32 [64], replicated, may hold values from 1.5 to 12
- balance: float32 [64, 64], replicated, may hold values from -0.75 to 0.75
Outputs:
- increment: float32 [64, 2048, 128], P('sect', ('date', 'blk')), parts along dimension 1
The draws below stay inside these ranges and needn't reach their ends.
There are 2 independent parts, one for each index of `date`. The reference program is written for one: setup_inputs(seed, part) draws one part's arguments, and reference() takes and returns one part's arrays. A program takes and returns all parts, laid end to end along the dimension named above; an argument that names none is the same for every part. Nothing has to cross between parts.
Inputs may be any that keep to these rules, and one draw needn't show every extreme that they name: `obs_count`: 512 is reached in every draw. `reach`: 0 and 3 both occur in every draw.
All inputs are finite; a program needn't handle non-finite values.
Results may differ from the reference program's by a relative error of at most 0.0029.
Values may be sent and summed in bfloat16 or wider, within the bound.
No kernel may reach another device: no remote copies, remote signals or barrier semaphores. Data moves between devices by JAX's collectives and lax.ppermute only.
A program may use at most 64 MiB of HBM per device.

```python
import math
import jax
import jax.numpy as jnp
from jax import lax

L = 64
C = 128
GX = 8
GY = 16
OBS_DEV = 512
REACH = 3
G_DEV = 128
BLOCKS = 8
SECTIONS = 2


def draw_obs_count(key, part):
    first_key, second_key = jax.random.split(jax.random.fold_in(key, 11))
    base_rows = jax.random.randint(first_key, (BLOCKS, SECTIONS), OBS_DEV // 16, OBS_DEV // 4 + 1)
    doublings = jax.random.randint(second_key, (BLOCKS, SECTIONS), 0, 3)
    counts = jnp.minimum(jnp.left_shift(base_rows, doublings), OBS_DEV)
    return counts.at[0, 0].set(OBS_DEV).astype(jnp.int32)


def draw_reach(key, part):
    spans = jax.random.randint(jax.random.fold_in(key, 23), (BLOCKS, 2), 0, REACH + 1)
    return spans.at[0, 0].set(REACH).at[0, 1].set(0).astype(jnp.int32)


def place_ends(array, rng, smallest, top_value):
    dims = array.shape
    index_at = [jax.random.randint(jax.random.fold_in(rng, axis), (), 0, dims[axis]) for axis in range(len(dims))]
    array = array.at[tuple(index_at)].set(smallest)
    longest = dims.index(max(dims))
    index_at[longest] = (index_at[longest] + 1) % dims[longest]
    return array.at[tuple(index_at)].set(top_value)


def levels(own_key, shape, cuts, smallest, high):
    gain = 1.0
    for dim, parts in cuts:
        steps = jax.random.uniform(jax.random.fold_in(jax.random.fold_in(own_key, 6), dim), (parts,), jnp.float32, smallest / len(cuts), high / len(cuts))
        gain = gain * jnp.repeat(jnp.exp(steps), shape[dim] // parts).reshape((-1,) + (1,) * (len(shape) - 1 - dim))
    return gain


def scatter_about(key, dims, deviation, most, shards=(), held_as=jnp.bfloat16):
    loudness = levels(key, dims, shards, -0.22, 0.18) if shards else 1.0
    drawn = jax.random.normal(key, dims, jnp.float32) * deviation * loudness
    return jnp.minimum(jnp.maximum(drawn, -most), most).astype(held_as)


def setup_inputs(seed: int = 0, part: int = 0) -> dict:
    key_of = jax.random.split(jax.random.key(seed), 12)
    part_keys = jax.random.split(jax.random.fold_in(key_of[11], part), 12)
    return {
        "obs_weight": scatter_about(part_keys[0], (BLOCKS, SECTIONS, OBS_DEV, C), 0.5, 4.0, ((0, 8), (1, 2))),
        "obs_frac": jnp.clip(1.0 * jax.random.uniform(part_keys[1], (BLOCKS, SECTIONS, 2, OBS_DEV), jnp.float32) ** levels(part_keys[1], (BLOCKS, SECTIONS, 2, OBS_DEV), ((0, 8), (1, 2)), -0.2, 0.2), 0.0, 1.0).astype(jnp.bfloat16),
        "obs_cell": place_ends(jax.random.randint(part_keys[2], (BLOCKS, SECTIONS, OBS_DEV), 0, G_DEV), jax.random.fold_in(part_keys[2], 1), 0, G_DEV - 1).astype(jnp.int32),
        "obs_level": place_ends(jax.random.randint(part_keys[3], (BLOCKS, SECTIONS, OBS_DEV), 0, L), jax.random.fold_in(part_keys[3], 1), 0, L - 1).astype(jnp.int32),
        "obs_count": draw_obs_count(jax.random.fold_in(jax.random.fold_in(key_of[11], part), 71), part),
        "reach": draw_reach(jax.random.fold_in(jax.random.fold_in(key_of[11], part), 71), part),
        "length_x": jnp.clip(jnp.exp(jax.random.uniform(key_of[6], (L,), jnp.float32, math.log(0.5), math.log(2.0))), 0.5, 2.0),
        "length_y": jnp.clip(jnp.exp(jax.random.uniform(key_of[7], (L,), jnp.float32, math.log(0.1), math.log(0.5))), 0.1, 0.5),
        "tilt": jnp.clip(jax.random.uniform(key_of[8], (L,), jnp.float32, -0.7, 0.7), -0.7, 0.7),
        "vert_len": jnp.clip(jnp.exp(jax.random.uniform(key_of[9], (L,), jnp.float32, math.log(1.5), math.log(12.0))), 1.5, 12.0),
        "balance": scatter_about(key_of[10], (L, L), L ** -0.5, 0.75, (), jnp.float32),
    }


def cover_tile(offset, fraction, cell_index, level_index, length_x, length_y, tilt, vert_len):
    column = jnp.arange(G_DEV, dtype=jnp.int32)
    grid_x = ((column // GY).astype(jnp.float32) + 0.5) / GX
    grid_y = ((column % GY).astype(jnp.float32) + 0.5) / GY
    obs_x = ((cell_index // GY).astype(jnp.float32) + fraction[0].astype(jnp.float32)) / GX
    obs_y = ((cell_index % GY).astype(jnp.float32) + fraction[1].astype(jnp.float32)) / GY
    east_gap = offset + grid_x[:, None] - obs_x[None, :]
    north_gap = grid_y[:, None] - obs_y[None, :]
    scaled_u = east_gap[None] / length_x[:, None, None]
    scaled_v = north_gap[None] / length_y[:, None, None]
    quadratic = scaled_u * scaled_u + scaled_v * scaled_v + 2.0 * tilt[:, None, None] * scaled_u * scaled_v
    horizontal = 1.0 / ((1.0 + quadratic) * (1.0 + quadratic))
    heights = jnp.arange(L, dtype=jnp.int32).astype(jnp.float32)
    separation = (heights[:, None] - level_index.astype(jnp.float32)[None, :]) / vert_len[:, None]
    vertical = 1.0 / (1.0 + separation * separation)
    return (horizontal * vertical[:, None, :]).astype(jnp.bfloat16)


def reference(obs_weight, obs_frac, obs_cell, obs_level, obs_count, reach, length_x, length_y, tilt, vert_len, balance):
    row_number = jnp.arange(OBS_DEV, dtype=jnp.int32)
    live = row_number[None, None, :] < obs_count[:, :, None]
    live_weight = jnp.where(live[..., None], obs_weight, jnp.zeros_like(obs_weight))

    def one_block(grid_block):
        running = jnp.zeros((L, G_DEV, C), jnp.float32)
        for offset in range(-REACH, REACH + 1):
            source = ((grid_block - offset) % BLOCKS).astype(jnp.int32)
            used = (offset <= reach[source, 1]) & (-offset <= reach[source, 0])
            for section in range(SECTIONS):
                tile = cover_tile(float(offset), obs_frac[source, section], obs_cell[source, section],
                                  obs_level[source, section], length_x, length_y, tilt, vert_len)
                term = jnp.einsum("lgo,oc->lgc", tile.astype(jnp.float32),
                                  live_weight[source, section].astype(jnp.float32),
                                  precision=lax.Precision.HIGHEST)
                running = running + jnp.where(used, term, jnp.zeros_like(term))
        return running

    analysis = lax.map(one_block, jnp.arange(BLOCKS, dtype=jnp.int32))
    analysis = jnp.transpose(analysis, (1, 0, 2, 3)).reshape(L, BLOCKS * G_DEV * C)
    increment = jnp.dot(balance, analysis, precision=lax.Precision.HIGHEST, preferred_element_type=jnp.float32)
    return increment.reshape(L, BLOCKS * G_DEV, C)
```

```python
import functools
import jax
import jax.numpy as jnp
from jax import lax
from jax.experimental import pallas as pl
from jax.experimental.pallas import tpu as pltpu
from jax.sharding import PartitionSpec as P

GX = 8
GY = 16
G_DEV = GX * GY
TILE = 128
QUAD = 4
GROUP = 16
F32 = jnp.float32
BF16 = jnp.bfloat16
VMEM = pl.BlockSpec(memory_space=pltpu.VMEM)
SMEM = pl.BlockSpec(memory_space=pltpu.SMEM)
PARAMS = pltpu.CompilerParams(vmem_limit_bytes=20 << 20)


def pack_kernel(count_ref, reach_ref, weight_ref, frac_ref, cell_ref, level_ref, out_ref):
    capacity = weight_ref.shape[2]
    chunks = capacity // TILE
    count = count_ref[0, 0]
    row = lax.broadcasted_iota(jnp.int32, (capacity, TILE), 0)
    weight = weight_ref[0, 0].astype(F32)
    out_ref[0:capacity, :] = jnp.where(row < count, weight, 0.0).astype(BF16)
    fraction = frac_ref[0, 0].astype(F32)
    cell = cell_ref[0].astype(F32)
    level = level_ref[0].astype(F32)
    rows = []
    for table in (fraction[0:1], fraction[1:2], cell, level):
        for i in range(chunks):
            rows.append(table[:, i * TILE : (i + 1) * TILE])
    out_ref[capacity : capacity + 4 * chunks, :] = jnp.concatenate(rows, 0).astype(BF16)
    live = (count + TILE - 1) // TILE
    code = live + 8 * (reach_ref[0, 0] + 4 * reach_ref[0, 1])
    tail = out_ref.shape[0] - capacity - 4 * chunks
    out_ref[capacity + 4 * chunks :, :] = jnp.full((tail, TILE), code, jnp.int32).astype(F32).astype(BF16)


def pack(obs_count, reach, obs_weight, obs_frac, obs_cell, obs_level):
    capacity = obs_weight.shape[2]
    rows = capacity + 4 * (capacity // TILE) + 16
    return pl.pallas_call(
        pack_kernel,
        out_shape=jax.ShapeDtypeStruct((rows, TILE), BF16),
        in_specs=[SMEM, SMEM, VMEM, VMEM, VMEM, VMEM],
        out_specs=VMEM,
        compiler_params=PARAMS,
    )(obs_count, reach, obs_weight, obs_frac, obs_cell, obs_level)


def gather_chunks(packets, offsets, capacity, w_all, ox_all, oy_all, le_all, order):
    chunks = capacity // TILE
    filled = jnp.int32(0)
    for i, (packet, offset) in enumerate(zip(packets, offsets)):
        w_all[i * capacity : (i + 1) * capacity, :] = packet[0:capacity, :]
        place = packet[capacity : capacity + 4 * chunks, :].astype(F32)
        fx, fy, cell, level = (place[t * chunks : (t + 1) * chunks] for t in range(4))
        cx = jnp.floor(cell * (1.0 / GY))
        cy = cell - cx * GY
        shift = jnp.full((1, TILE), offset, jnp.int32).astype(F32)
        ox_all[i * chunks : (i + 1) * chunks, :] = (cx + fx) * (1.0 / GX) - shift
        oy_all[i * chunks : (i + 1) * chunks, :] = (cy + fy) * (1.0 / GY)
        le_all[i * chunks : (i + 1) * chunks, :] = level
        tail = packet[capacity + 4 * chunks :, :].astype(F32)
        code = jnp.max(tail).astype(jnp.int32)
        live = code & 7
        below = (code >> 3) & 3
        above = (code >> 5) & 3
        used = jnp.where((offset <= above) & (-offset <= below), live, 0)
        for c in range(chunks):
            order[filled + c] = i * chunks + c
        filled = filled + used
    blank = len(packets) * chunks
    w_all[blank * TILE : (blank + 1) * TILE, :] = jnp.zeros((TILE, TILE), BF16)
    for ref in (ox_all, oy_all, le_all):
        ref[blank : blank + 8, :] = jnp.zeros((8, TILE), F32)
    for c in range(QUAD - 1):
        order[filled + c] = blank
    return filled


def spread(filled, lx, ly, tl, vl, acc, w_all, ox_all, oy_all, le_all, order, wq, sx, sy, sz, st, xs):
    levels = lx.shape[1]
    width = QUAD * TILE

    def column(ref):
        return jnp.transpose(jnp.broadcast_to(ref[...], (8, levels)))[:, 0:1]

    inv_x = 1.0 / column(lx)
    inv_y = 1.0 / column(ly)
    tilt = column(tl)
    inv_v = 1.0 / column(vl)
    height = lax.broadcasted_iota(jnp.int32, (levels, 1), 0).astype(F32)
    grid_x = (lax.broadcasted_iota(jnp.int32, (GX, 1), 0).astype(F32) + 0.5) / GX
    grid_y = (lax.broadcasted_iota(jnp.int32, (GY, 1), 0).astype(F32) + 0.5) / GY

    def quad(q, _):
        picks = [order[q * QUAD + i] for i in range(QUAD)]
        for i, r in enumerate(picks):
            wq[i * TILE : (i + 1) * TILE, :] = w_all[pl.ds(pl.multiple_of(r * TILE, TILE), TILE), :]

        def lanes(ref):
            return jnp.concatenate([ref[pl.ds(r, 1), :] for r in picks], 1)

        dx = grid_x - lanes(ox_all)
        dy = grid_y - lanes(oy_all)
        dy2 = dy * dy
        sep = (height - lanes(le_all)) * inv_v
        root = lax.rsqrt(lax.rsqrt(1.0 + sep * sep))
        full = root * root
        sx[...] = root * inv_x
        sy[...] = root * (tilt * inv_y)
        st[...] = full
        sz[...] = full * ((1.0 - tilt * tilt) * inv_y * inv_y)

        def group(g, _):
            first = g * GROUP
            rows = []
            for u in range(GROUP):
                l = first + u
                xs[u * GX : (u + 1) * GX, :] = dx * sx[pl.ds(l, 1), :]
                yv = dy * sy[pl.ds(l, 1), :]
                zv = dy2 * sz[pl.ds(l, 1), :] + st[pl.ds(l, 1), :]
                for i in range(GX):
                    a = xs[u * GX + i : u * GX + i + 1, :] + yv
                    y = a * a + zv
                    rows.append((1.0 / (y * y)).astype(BF16))
            cover = jnp.concatenate(rows, 0)
            at = pl.ds(pl.multiple_of(first * G_DEV, G_DEV), GROUP * G_DEV)
            acc[at, :] += jnp.dot(cover, wq[...], preferred_element_type=F32)
            return 0

        lax.fori_loop(0, levels // GROUP, group, 0)
        return 0

    lax.fori_loop(0, (filled + QUAD - 1) // QUAD, quad, 0)


def balance_step(balance, acc, own, other):
    levels = balance.shape[0]
    half = levels // 2
    mine = lax.axis_index("sect")
    matrix = jnp.concatenate(
        [
            balance[pl.ds(pl.multiple_of(mine * half, half), half), :],
            balance[pl.ds(pl.multiple_of((1 - mine) * half, half), half), :],
        ],
        0,
    )
    high = matrix.astype(BF16)
    low = (matrix - high.astype(F32)).astype(BF16)
    left = jnp.concatenate([high, low, high], 1)

    def column(i, _):
        for u in range(8):
            j = i * 8 + u
            value = acc[pl.ds(j, levels, stride=G_DEV), :]
            big = value.astype(BF16)
            small = (value - big.astype(F32)).astype(BF16)
            right = jnp.concatenate([big, big, small], 0)
            result = jnp.dot(left, right, preferred_element_type=F32)
            own[j] = result[0:half]
            other[j] = result[half:].astype(BF16)
        return 0

    lax.fori_loop(0, G_DEV // 8, column, 0)


def main_kernel(*refs, hops, capacity, first, last):
    refs = list(refs)
    lx, ly, tl, vl = refs[:4]
    refs = refs[4:]
    if not first:
        refs.pop(0)
    packets = refs[: len(hops)]
    refs = refs[len(hops) :]
    balance = refs.pop(0) if last else None
    acc = refs.pop(0)
    if last:
        own, other = refs[:2]
        refs = refs[2:]
    w_all, ox_all, oy_all, le_all, order, wq, sx, sy, sz, st, xs = refs[:11]
    if first:
        acc[...] = jnp.zeros(acc.shape, F32)
    parity = lax.rem(lax.axis_index("blk"), 2)
    offsets = [even if even == odd else jnp.where(parity == 0, even, odd) for even, odd in hops]
    filled = gather_chunks(packets, offsets, capacity, w_all, ox_all, oy_all, le_all, order)
    spread(filled, lx, ly, tl, vl, acc, w_all, ox_all, oy_all, le_all, order, wq, sx, sy, sz, st, xs)
    if last:
        balance_step(balance, acc, own, other)


def main_call(scales, acc, packets, hops, capacity, levels, balance=None):
    first = acc is None
    last = balance is not None
    chunks = capacity // TILE
    slots = len(hops) * chunks + 8
    operands = list(scales)
    aliases = {}
    if not first:
        aliases = {len(operands): 0}
        operands.append(acc)
    operands += list(packets)
    out_shape = [jax.ShapeDtypeStruct((levels * G_DEV, TILE), F32)]
    if last:
        operands.append(balance)
        half = levels // 2
        out_shape.append(jax.ShapeDtypeStruct((G_DEV, half, TILE), F32))
        out_shape.append(jax.ShapeDtypeStruct((G_DEV, half, TILE), BF16))
    width = QUAD * TILE
    scratch = [pltpu.VMEM(((len(hops) * chunks + 1) * TILE, TILE), BF16)]
    scratch += [pltpu.VMEM((slots, TILE), F32)] * 3
    scratch += [pltpu.SMEM((slots + QUAD,), jnp.int32), pltpu.VMEM((width, TILE), BF16)]
    scratch += [pltpu.VMEM((levels, width), F32)] * 4
    scratch += [pltpu.VMEM((GROUP * GX, width), F32)]
    return pl.pallas_call(
        functools.partial(main_kernel, hops=hops, capacity=capacity, first=first, last=last),
        out_shape=out_shape,
        in_specs=[VMEM] * len(operands),
        out_specs=[VMEM] * len(out_shape),
        scratch_shapes=scratch,
        input_output_aliases=aliases,
        compiler_params=PARAMS,
    )(*operands)


def finish_kernel(own, other, out):
    def column(i, _):
        for u in range(8):
            j = i * 8 + u
            out[pl.ds(j, own.shape[1], stride=G_DEV), :] = own[j] + other[j].astype(F32)
        return 0

    lax.fori_loop(0, G_DEV // 8, column, 0)


def shards(
    obs_weight,
    obs_frac,
    obs_cell,
    obs_level,
    obs_count,
    reach,
    length_x,
    length_y,
    tilt,
    vert_len,
    balance,
):
    levels = balance.shape[0]
    capacity = obs_weight.shape[2]
    blocks = lax.axis_size("blk")
    packet = pack(obs_count, reach, obs_weight, obs_frac, obs_cell, obs_level)
    scales = [v.reshape(1, levels) for v in (length_x, length_y, tilt, vert_len)]

    def move(value, where):
        return lax.ppermute(value, "blk", [(i, where(i) % blocks) for i in range(blocks)])

    def swap(i):
        return i + 1 if i % 2 == 0 else i - 1

    cross = move(packet, lambda i: i - 3 if i % 2 == 0 else i + 3)
    up = move(packet, lambda i: i + 2)
    down = move(packet, lambda i: i - 2)
    near = move(packet, swap)
    near_up = move(up, swap)
    near_down = move(down, swap)
    acc, = main_call(scales, None, (packet,), ((0, 0),), capacity, levels)
    acc, = main_call(scales, acc, (up, down, near), ((2, 2), (-2, -2), (-1, 1)), capacity, levels)
    _, own, other = main_call(
        scales, acc, (cross, near_up, near_down), ((3, -3), (1, 3), (-3, -1)), capacity, levels, balance
    )
    arrived = lax.ppermute(other, "sect", [(0, 1), (1, 0)])
    half = levels // 2
    out = pl.pallas_call(
        finish_kernel,
        out_shape=jax.ShapeDtypeStruct((half * G_DEV, TILE), F32),
        in_specs=[VMEM, VMEM],
        out_specs=VMEM,
        compiler_params=PARAMS,
    )(own, arrived)
    return out.reshape(half, G_DEV, TILE)


def solution(mesh):
    placed = (
        P(("date", "blk"), "sect", None, None),
        P(("date", "blk"), "sect", None, None),
        P(("date", "blk"), "sect", None),
        P(("date", "blk"), "sect", None),
        P(("date", "blk"), "sect"),
        P(("date", "blk"), None),
        P(),
        P(),
        P(),
        P(),
        P(),
    )
    return jax.shard_map(
        shards,
        mesh=mesh,
        in_specs=placed,
        out_specs=P("sect", ("date", "blk"), None),
        check_vma=False,
    )
```

```python
import functools
import jax
import jax.numpy as jnp
from jax import lax
from jax.experimental import pallas as pl
from jax.experimental.pallas import tpu as pltpu
from jax.sharding import PartitionSpec as P

GX = 8
GY = 16
G_DEV = GX * GY
TILE = 128
JOIN = 2
GROUP = 16
F32 = jnp.float32
BF16 = jnp.bfloat16
VMEM = pl.BlockSpec(memory_space=pltpu.VMEM)
SMEM = pl.BlockSpec(memory_space=pltpu.SMEM)
PARAMS = pltpu.CompilerParams(vmem_limit_bytes=20 << 20)


def pack_kernel(
    count_ref,
    reach_hbm,
    weight_hbm,
    frac_hbm,
    cell_hbm,
    level_hbm,
    lx_hbm,
    ly_hbm,
    tl_hbm,
    vl_hbm,
    balance_hbm,
    out_ref,
    scale_ref,
    left_ref,
    reach_ref,
    weight_ref,
    frac_ref,
    cell_ref,
    level_ref,
    lx_ref,
    ly_ref,
    tl_ref,
    vl_ref,
    balance_ref,
    sems,
):
    pairs = (
        (weight_hbm, weight_ref),
        (frac_hbm, frac_ref),
        (cell_hbm, cell_ref),
        (level_hbm, level_ref),
        (reach_hbm, reach_ref),
        (lx_hbm, lx_ref),
        (ly_hbm, ly_ref),
        (tl_hbm, tl_ref),
        (vl_hbm, vl_ref),
        (balance_hbm, balance_ref),
    )
    copies = [pltpu.make_async_copy(src, dst, sems.at[i]) for i, (src, dst) in enumerate(pairs)]
    for copy in copies:
        copy.start()
    for copy in copies:
        copy.wait()
    capacity = weight_ref.shape[2]
    chunks = capacity // TILE
    levels = lx_ref.shape[1]
    half = levels // 2
    count = count_ref[0, 0]
    row = lax.broadcasted_iota(jnp.int32, (capacity, TILE), 0)
    weight = weight_ref[0, 0].astype(F32)
    out_ref[0:capacity, :] = jnp.where(row < count, weight, 0.0).astype(BF16)
    fraction = frac_ref[0, 0].astype(F32)
    cell = cell_ref[0].astype(F32)
    level = level_ref[0].astype(F32)
    rows = []
    for table in (fraction[0:1], fraction[1:2], cell, level):
        for i in range(chunks):
            rows.append(table[:, i * TILE : (i + 1) * TILE])
    out_ref[capacity : capacity + 4 * chunks, :] = jnp.concatenate(rows, 0).astype(BF16)
    live = (count + TILE - 1) // TILE
    code = live + 8 * (reach_ref[0, 0] + 4 * reach_ref[0, 1])
    tail = out_ref.shape[0] - capacity - 4 * chunks
    out_ref[capacity + 4 * chunks :, :] = jnp.full((tail, TILE), code, jnp.int32).astype(F32).astype(BF16)
    inv_x = 1.0 / lx_ref[...]
    inv_y = 1.0 / ly_ref[...]
    tilt = tl_ref[...]
    lines = [inv_x, tilt * inv_y, (1.0 - tilt * tilt) * inv_y * inv_y, 1.0 / vl_ref[...]]
    scale_ref[...] = jnp.transpose(jnp.concatenate(lines + lines, 0))
    mine = lax.axis_index("sect")
    matrix = jnp.concatenate(
        [
            balance_ref[pl.ds(pl.multiple_of(mine * half, half), half), :],
            balance_ref[pl.ds(pl.multiple_of((1 - mine) * half, half), half), :],
        ],
        0,
    )
    high = matrix.astype(BF16)
    low = (matrix - high.astype(F32)).astype(BF16)
    left_ref[...] = jnp.concatenate([high, low, high], 1)


def pack(obs_count, reach, obs_weight, obs_frac, obs_cell, obs_level, scales, balance):
    capacity = obs_weight.shape[2]
    levels = balance.shape[0]
    rows = capacity + 4 * (capacity // TILE) + 16
    operands = [obs_count, reach, obs_weight, obs_frac, obs_cell, obs_level, *scales, balance]
    operands[1:] = [pltpu.with_memory_space_constraint(v, pltpu.HBM) for v in operands[1:]]
    spaces = [pltpu.SMEM] + [pltpu.VMEM] * 9
    return pl.pallas_call(
        pack_kernel,
        out_shape=(
            jax.ShapeDtypeStruct((rows, TILE), BF16),
            jax.ShapeDtypeStruct((levels, 8), F32),
            jax.ShapeDtypeStruct((levels, 3 * levels), BF16),
        ),
        in_specs=[SMEM] + [pl.BlockSpec(memory_space=pltpu.HBM)] * (len(operands) - 1),
        out_specs=(VMEM, VMEM, VMEM),
        scratch_shapes=[space(v.shape, v.dtype) for space, v in zip(spaces, operands[1:])]
        + [pltpu.SemaphoreType.DMA((len(operands) - 1,))],
        compiler_params=PARAMS,
    )(*operands)


def gather_chunks(packets, offsets, capacity, w_all, ox_all, oy_all, le_all, order):
    chunks = capacity // TILE
    filled = jnp.int32(0)
    for i, (packet, offset) in enumerate(zip(packets, offsets)):
        w_all[i * capacity : (i + 1) * capacity, :] = packet[0:capacity, :]
        place = packet[capacity : capacity + 4 * chunks, :].astype(F32)
        fx, fy, cell, level = (place[t * chunks : (t + 1) * chunks] for t in range(4))
        cx = jnp.floor(cell * (1.0 / GY))
        cy = cell - cx * GY
        shift = jnp.full((1, TILE), offset, jnp.int32).astype(F32)
        ox_all[i * chunks : (i + 1) * chunks, :] = (cx + fx) * (1.0 / GX) - shift
        oy_all[i * chunks : (i + 1) * chunks, :] = (cy + fy) * (1.0 / GY)
        le_all[i * chunks : (i + 1) * chunks, :] = level
        tail = packet[capacity + 4 * chunks :, :].astype(F32)
        code = jnp.max(tail).astype(jnp.int32)
        live = code & 7
        below = (code >> 3) & 3
        above = (code >> 5) & 3
        used = jnp.where((offset <= above) & (-offset <= below), live, 0)
        for c in range(chunks):
            order[filled + c] = i * chunks + c
        filled = filled + used
    blank = len(packets) * chunks
    w_all[blank * TILE : (blank + 1) * TILE, :] = jnp.zeros((TILE, TILE), BF16)
    for ref in (ox_all, oy_all, le_all):
        ref[blank : blank + 8, :] = jnp.zeros((8, TILE), F32)
    for c in range(JOIN - 1):
        order[filled + c] = blank
    return filled


def spread(filled, scale, acc, w_all, ox_all, oy_all, le_all, order, wq, dxs, dys, dzs, sx, ys, zs):
    levels = scale.shape[0]
    inv_x = scale[:, 0:1]
    tilt_y = scale[:, 1:2]
    rest_y = scale[:, 2:3]
    inv_v = scale[:, 3:4]
    height = lax.broadcasted_iota(jnp.int32, (levels, 1), 0).astype(F32)
    grid_x = (lax.broadcasted_iota(jnp.int32, (GX, 1), 0).astype(F32) + 0.5) / GX
    grid_y = (lax.broadcasted_iota(jnp.int32, (GY, 1), 0).astype(F32) + 0.5) / GY

    def join(q, _):
        picks = [order[q * JOIN + i] for i in range(JOIN)]
        for i, r in enumerate(picks):
            wq[i * TILE : (i + 1) * TILE, :] = w_all[pl.ds(pl.multiple_of(r * TILE, TILE), TILE), :]

        def lanes(ref):
            return jnp.concatenate([ref[pl.ds(r, 1), :] for r in picks], 1)

        dxs[...] = grid_x - lanes(ox_all)
        dy = grid_y - lanes(oy_all)
        dys[...] = dy
        dzs[...] = dy * dy
        sep = (height - lanes(le_all)) * inv_v
        root = lax.rsqrt(lax.rsqrt(1.0 + sep * sep))
        full = root * root
        sx[...] = root * inv_x
        sy = root * tilt_y
        sz = full * rest_y
        for i in range(GY):
            ys[i] = sy * dys[i : i + 1, :]
            zs[i] = sz * dzs[i : i + 1, :] + full
        right = wq[...]
        for first in range(0, levels, GROUP):
            span = slice(first, first + GROUP)
            rows = []
            for i in range(GX):
                xv = sx[span, :] * dxs[i : i + 1, :]
                for j in range(GY):
                    a = xv + ys[j, span, :]
                    y = a * a + zs[j, span, :]
                    rows.append((1.0 / (y * y)).astype(BF16))
            term = jnp.dot(jnp.concatenate(rows, 0), right, preferred_element_type=F32)
            for j in range(G_DEV):
                at = slice(j * levels + first, j * levels + first + GROUP)
                acc[at, :] += term[j * GROUP : (j + 1) * GROUP]
        return 0

    lax.fori_loop(0, (filled + JOIN - 1) // JOIN, join, 0)


def balance_step(left_ref, acc, own, other):
    levels = left_ref.shape[0]
    half = levels // 2
    left = left_ref[...]
    steps = 32

    def columns(i, _):
        for u in range(steps):
            j = (i * steps + u) * 2
            value = jnp.concatenate(
                [acc[pl.ds(pl.multiple_of((j + n) * levels, levels), levels), :] for n in range(2)], 1
            )
            big = value.astype(BF16)
            small = (value - big.astype(F32)).astype(BF16)
            right = jnp.concatenate([big, big, small], 0)
            result = jnp.dot(left, right, preferred_element_type=F32)
            for n in range(2):
                own[j + n] = result[0:half, n * TILE : (n + 1) * TILE]
                other[j + n] = result[half:, n * TILE : (n + 1) * TILE].astype(BF16)
        return 0

    lax.fori_loop(0, G_DEV // (2 * steps), columns, 0)


def main_kernel(*refs, hops, capacity, first, last):
    refs = list(refs)
    scale = refs.pop(0)
    if not first:
        refs.pop(0)
    packets = refs[: len(hops)]
    refs = refs[len(hops) :]
    left = refs.pop(0) if last else None
    acc = refs.pop(0)
    if last:
        own, other = refs[:2]
        refs = refs[2:]
    if first:
        acc[...] = jnp.zeros(acc.shape, F32)
    parity = lax.rem(lax.axis_index("blk"), 2)
    offsets = [even if even == odd else jnp.where(parity == 0, even, odd) for even, odd in hops]
    filled = gather_chunks(packets, offsets, capacity, *refs[:5])
    spread(filled, scale, acc, *refs)
    if last:
        balance_step(left, acc, own, other)


def main_call(scale, acc, packets, hops, capacity, left=None):
    first = acc is None
    last = left is not None
    levels = scale.shape[0]
    chunks = capacity // TILE
    slots = len(hops) * chunks + 8
    operands = [scale]
    aliases = {}
    if not first:
        aliases = {1: 0}
        operands.append(acc)
    operands += list(packets)
    out_shape = [jax.ShapeDtypeStruct((levels * G_DEV, TILE), F32)]
    if last:
        operands.append(left)
        half = levels // 2
        out_shape.append(jax.ShapeDtypeStruct((G_DEV, half, TILE), F32))
        out_shape.append(jax.ShapeDtypeStruct((G_DEV, half, TILE), BF16))
    width = JOIN * TILE
    scratch = [pltpu.VMEM(((len(hops) * chunks + 1) * TILE, TILE), BF16)]
    scratch += [pltpu.VMEM((slots, TILE), F32)] * 3
    scratch += [pltpu.SMEM((slots + JOIN,), jnp.int32), pltpu.VMEM((width, TILE), BF16)]
    scratch += [pltpu.VMEM((n, width), F32) for n in (GX, GY, GY, levels)]
    scratch += [pltpu.VMEM((GY, levels, width), F32)] * 2
    return pl.pallas_call(
        functools.partial(main_kernel, hops=hops, capacity=capacity, first=first, last=last),
        out_shape=out_shape,
        in_specs=[VMEM] * len(operands),
        out_specs=[VMEM] * len(out_shape),
        scratch_shapes=scratch,
        input_output_aliases=aliases,
        compiler_params=PARAMS,
    )(*operands)


def finish_kernel(own, other, out, total, sems):
    parts = sems.shape[0]
    width = G_DEV // parts
    copies = []
    for p in range(parts):
        for j in range(p * width, (p + 1) * width):
            total[j] = own[j] + other[j].astype(F32)
        for j in range(p * width, (p + 1) * width):
            copies.append(pltpu.make_async_copy(total.at[j], out.at[:, j, :], sems.at[j // width]))
            copies[-1].start()
    for copy in copies:
        copy.wait()


def shards(
    obs_weight,
    obs_frac,
    obs_cell,
    obs_level,
    obs_count,
    reach,
    length_x,
    length_y,
    tilt,
    vert_len,
    balance,
):
    levels = balance.shape[0]
    capacity = obs_weight.shape[2]
    blocks = lax.axis_size("blk")
    scales = [v.reshape(1, levels) for v in (length_x, length_y, tilt, vert_len)]
    packet, scale, left = pack(
        obs_count, reach, obs_weight, obs_frac, obs_cell, obs_level, scales, balance
    )

    def move(value, where):
        return lax.ppermute(value, "blk", [(i, where(i) % blocks) for i in range(blocks)])

    def swap(i):
        return i + 1 if i % 2 == 0 else i - 1

    cross = move(packet, lambda i: i - 3 if i % 2 == 0 else i + 3)
    up = move(packet, lambda i: i + 2)
    down = move(packet, lambda i: i - 2)
    near = move(packet, swap)
    (acc,) = main_call(scale, None, (packet,), ((0, 0),), capacity)
    up, down, acc = lax.optimization_barrier((up, down, acc))
    near_up = move(up, swap)
    near_down = move(down, swap)
    (acc,) = main_call(scale, acc, (up, down, near), ((2, 2), (-2, -2), (-1, 1)), capacity)
    _, own, other = main_call(
        scale, acc, (cross, near_up, near_down), ((3, -3), (1, 3), (-3, -1)), capacity, left
    )
    arrived = lax.ppermute(other, "sect", [(0, 1), (1, 0)])
    half = levels // 2
    return pl.pallas_call(
        finish_kernel,
        out_shape=jax.ShapeDtypeStruct((half, G_DEV, TILE), F32),
        in_specs=[VMEM, VMEM],
        out_specs=pl.BlockSpec(memory_space=pltpu.HBM),
        scratch_shapes=[pltpu.VMEM((G_DEV, half, TILE), F32), pltpu.SemaphoreType.DMA((8,))],
        compiler_params=PARAMS,
    )(own, arrived)


def solution(mesh):
    placed = (
        P(("date", "blk"), "sect", None, None),
        P(("date", "blk"), "sect", None, None),
        P(("date", "blk"), "sect", None),
        P(("date", "blk"), "sect", None),
        P(("date", "blk"), "sect"),
        P(("date", "blk"), None),
        P(),
        P(),
        P(),
        P(),
        P(),
    )
    return jax.shard_map(
        shards,
        mesh=mesh,
        in_specs=placed,
        out_specs=P("sect", ("date", "blk"), None),
        check_vma=False,
    )
```

```python
import functools
import jax
import jax.numpy as jnp
from jax import lax
from jax.experimental import pallas as pl
from jax.experimental.pallas import tpu as pltpu
from jax.sharding import PartitionSpec as P

GX = 8
GY = 16
G_DEV = GX * GY
TILE = 128
HALF = GY // 2
G_OWN = GX * HALF
JOIN = 2
GROUP = 16
F32 = jnp.float32
BF16 = jnp.bfloat16
VMEM = pl.BlockSpec(memory_space=pltpu.VMEM)
SMEM = pl.BlockSpec(memory_space=pltpu.SMEM)
PARAMS = pltpu.CompilerParams(vmem_limit_bytes=20 << 20)


def pack_kernel(
    count_ref,
    reach_hbm,
    weight_hbm,
    frac_hbm,
    cell_hbm,
    level_hbm,
    lx_hbm,
    ly_hbm,
    tl_hbm,
    vl_hbm,
    balance_hbm,
    out_ref,
    scale_ref,
    left_ref,
    reach_ref,
    weight_ref,
    frac_ref,
    cell_ref,
    level_ref,
    lx_ref,
    ly_ref,
    tl_ref,
    vl_ref,
    balance_ref,
    sems,
):
    pairs = (
        (weight_hbm, weight_ref),
        (frac_hbm, frac_ref),
        (cell_hbm, cell_ref),
        (level_hbm, level_ref),
        (reach_hbm, reach_ref),
        (lx_hbm, lx_ref),
        (ly_hbm, ly_ref),
        (tl_hbm, tl_ref),
        (vl_hbm, vl_ref),
        (balance_hbm, balance_ref),
    )
    copies = [pltpu.make_async_copy(src, dst, sems.at[i]) for i, (src, dst) in enumerate(pairs)]
    for copy in copies:
        copy.start()
    for copy in copies:
        copy.wait()
    capacity = weight_ref.shape[2]
    chunks = capacity // TILE
    levels = lx_ref.shape[1]
    half = levels // 2
    count = count_ref[0, 0]
    row = lax.broadcasted_iota(jnp.int32, (capacity, TILE), 0)
    weight = weight_ref[0, 0].astype(F32)
    out_ref[0:capacity, :] = jnp.where(row < count, weight, 0.0).astype(BF16)
    fraction = frac_ref[0, 0].astype(F32)
    cell = cell_ref[0].astype(F32)
    level = level_ref[0].astype(F32)
    rows = []
    for table in (fraction[0:1], fraction[1:2], cell, level):
        for i in range(chunks):
            rows.append(table[:, i * TILE : (i + 1) * TILE])
    out_ref[capacity : capacity + 4 * chunks, :] = jnp.concatenate(rows, 0).astype(BF16)
    live = (count + TILE - 1) // TILE
    code = live + 8 * (reach_ref[0, 0] + 4 * reach_ref[0, 1])
    tail = out_ref.shape[0] - capacity - 4 * chunks
    out_ref[capacity + 4 * chunks :, :] = jnp.full((tail, TILE), code, jnp.int32).astype(F32).astype(BF16)
    inv_x = 1.0 / lx_ref[...]
    inv_y = 1.0 / ly_ref[...]
    tilt = tl_ref[...]
    lines = [inv_x, tilt * inv_y, (1.0 - tilt * tilt) * inv_y * inv_y, 1.0 / vl_ref[...]]
    scale_ref[...] = jnp.transpose(jnp.concatenate(lines + lines, 0))
    mine = lax.axis_index("sect")
    matrix = jnp.concatenate(
        [
            balance_ref[pl.ds(pl.multiple_of(mine * half, half), half), :],
            balance_ref[pl.ds(pl.multiple_of((1 - mine) * half, half), half), :],
        ],
        0,
    )
    high = matrix.astype(BF16)
    low = (matrix - high.astype(F32)).astype(BF16)
    left_ref[...] = jnp.concatenate([high, low, high], 1)


def pack(obs_count, reach, obs_weight, obs_frac, obs_cell, obs_level, scales, balance):
    capacity = obs_weight.shape[2]
    levels = balance.shape[0]
    rows = capacity + 4 * (capacity // TILE) + 16
    operands = [obs_count, reach, obs_weight, obs_frac, obs_cell, obs_level, *scales, balance]
    operands[1:] = [pltpu.with_memory_space_constraint(v, pltpu.HBM) for v in operands[1:]]
    spaces = [pltpu.SMEM] + [pltpu.VMEM] * 9
    return pl.pallas_call(
        pack_kernel,
        out_shape=(
            jax.ShapeDtypeStruct((rows, TILE), BF16),
            jax.ShapeDtypeStruct((levels, 8), F32),
            jax.ShapeDtypeStruct((levels, 3 * levels), BF16),
        ),
        in_specs=[SMEM] + [pl.BlockSpec(memory_space=pltpu.HBM)] * (len(operands) - 1),
        out_specs=(VMEM, VMEM, VMEM),
        scratch_shapes=[space(v.shape, v.dtype) for space, v in zip(spaces, operands[1:])]
        + [pltpu.SemaphoreType.DMA((len(operands) - 1,))],
        compiler_params=PARAMS,
    )(*operands)


def gather_chunks(packets, offsets, capacity, w_all, ox_all, oy_all, le_all, order):
    chunks = capacity // TILE
    filled = jnp.int32(0)
    for i, (packet, offset) in enumerate(zip(packets, offsets)):
        w_all[i * capacity : (i + 1) * capacity, :] = packet[0:capacity, :]
        place = packet[capacity : capacity + 4 * chunks, :].astype(F32)
        fx, fy, cell, level = (place[t * chunks : (t + 1) * chunks] for t in range(4))
        cx = jnp.floor(cell * (1.0 / GY))
        cy = cell - cx * GY
        shift = jnp.full((1, TILE), offset, jnp.int32).astype(F32)
        ox_all[i * chunks : (i + 1) * chunks, :] = (cx + fx) * (1.0 / GX) - shift
        oy_all[i * chunks : (i + 1) * chunks, :] = (cy + fy) * (1.0 / GY)
        le_all[i * chunks : (i + 1) * chunks, :] = level
        tail = packet[capacity + 4 * chunks :, :].astype(F32)
        code = jnp.max(tail).astype(jnp.int32)
        live = code & 7
        below = (code >> 3) & 3
        above = (code >> 5) & 3
        used = jnp.where((offset <= above) & (-offset <= below), live, 0)
        for c in range(chunks):
            order[filled + c] = i * chunks + c
        filled = filled + used
    blank = len(packets) * chunks
    w_all[blank * TILE : (blank + 1) * TILE, :] = jnp.zeros((TILE, TILE), BF16)
    for ref in (ox_all, oy_all, le_all):
        ref[blank : blank + 8, :] = jnp.zeros((8, TILE), F32)
    for c in range(JOIN - 1):
        order[filled + c] = blank
    return filled


def spread(filled, scale, acc, w_all, ox_all, oy_all, le_all, order, wq, dxs, dys, dzs, sx, ys, zs):
    levels = scale.shape[0]
    inv_x = scale[:, 0:1]
    tilt_y = scale[:, 1:2]
    rest_y = scale[:, 2:3]
    inv_v = scale[:, 3:4]
    height = lax.broadcasted_iota(jnp.int32, (levels, 1), 0).astype(F32)
    grid_x = (lax.broadcasted_iota(jnp.int32, (GX, 1), 0).astype(F32) + 0.5) / GX
    lower = lax.axis_index("sect") * HALF
    grid_y = ((lax.broadcasted_iota(jnp.int32, (HALF, 1), 0) + lower).astype(F32) + 0.5) / GY

    def join(q, _):
        picks = [order[q * JOIN + i] for i in range(JOIN)]
        for i, r in enumerate(picks):
            wq[i * TILE : (i + 1) * TILE, :] = w_all[pl.ds(pl.multiple_of(r * TILE, TILE), TILE), :]

        def lanes(ref):
            return jnp.concatenate([ref[pl.ds(r, 1), :] for r in picks], 1)

        dxs[...] = grid_x - lanes(ox_all)
        dy = grid_y - lanes(oy_all)
        dys[...] = dy
        dzs[...] = dy * dy
        sep = (height - lanes(le_all)) * inv_v
        root = lax.rsqrt(lax.rsqrt(1.0 + sep * sep))
        full = root * root
        sx[...] = root * inv_x
        sy = root * tilt_y
        sz = full * rest_y
        for i in range(HALF):
            ys[i] = sy * dys[i : i + 1, :]
            zs[i] = sz * dzs[i : i + 1, :] + full
        right = wq[...]
        for first in range(0, levels, GROUP):
            span = slice(first, first + GROUP)
            rows = []
            for i in range(GX):
                xv = sx[span, :] * dxs[i : i + 1, :]
                for j in range(HALF):
                    a = xv + ys[j, span, :]
                    y = a * a + zs[j, span, :]
                    rows.append((1.0 / (y * y)).astype(BF16))
            term = jnp.dot(jnp.concatenate(rows, 0), right, preferred_element_type=F32)
            for j in range(G_OWN):
                at = slice(j * levels + first, j * levels + first + GROUP)
                acc[at, :] += term[j * GROUP : (j + 1) * GROUP]
        return 0

    lax.fori_loop(0, (filled + JOIN - 1) // JOIN, join, 0)


def balance_step(left_ref, acc, out, other, own, sems):
    levels = left_ref.shape[0]
    half = levels // 2
    left = left_ref[...]
    lower = lax.axis_index("sect") * HALF
    copies = []
    for j in range(0, G_OWN, 2):
        value = jnp.concatenate([acc[(j + n) * levels : (j + n + 1) * levels, :] for n in range(2)], 1)
        big = value.astype(BF16)
        small = (value - big.astype(F32)).astype(BF16)
        right = jnp.concatenate([big, big, small], 0)
        result = jnp.dot(left, right, preferred_element_type=F32)
        for n in range(2):
            own[j + n] = result[0:half, n * TILE : (n + 1) * TILE]
            other[j + n] = result[half:, n * TILE : (n + 1) * TILE].astype(BF16)
    for j in range(G_OWN):
        column = (j // HALF) * GY + lower + j % HALF
        copies.append(pltpu.make_async_copy(own.at[j], out.at[:, column, :], sems.at[j // HALF]))
        copies[-1].start()
    for copy in copies:
        copy.wait()


def main_kernel(*refs, hops, capacity, first, last):
    refs = list(refs)
    scale = refs.pop(0)
    if not first:
        refs.pop(0)
    packets = refs[: len(hops)]
    refs = refs[len(hops) :]
    left = refs.pop(0) if last else None
    acc = refs.pop(0)
    if last:
        out, other = refs[:2]
        own, sems = refs[-2:]
        refs = refs[2:-2]
    if first:
        acc[...] = jnp.zeros(acc.shape, F32)
    parity = lax.rem(lax.axis_index("blk"), 2)
    offsets = [even if even == odd else jnp.where(parity == 0, even, odd) for even, odd in hops]
    filled = gather_chunks(packets, offsets, capacity, *refs[:5])
    spread(filled, scale, acc, *refs)
    if last:
        balance_step(left, acc, out, other, own, sems)


def main_call(scale, acc, packets, hops, capacity, left=None):
    first = acc is None
    last = left is not None
    levels = scale.shape[0]
    chunks = capacity // TILE
    slots = len(hops) * chunks + 8
    operands = [scale]
    aliases = {}
    if not first:
        aliases = {1: 0}
        operands.append(acc)
    operands += list(packets)
    out_shape = [jax.ShapeDtypeStruct((levels * G_OWN, TILE), F32)]
    out_specs = [VMEM]
    if last:
        operands.append(left)
        half = levels // 2
        out_shape.append(jax.ShapeDtypeStruct((half, G_DEV, TILE), F32))
        out_shape.append(jax.ShapeDtypeStruct((G_OWN, half, TILE), BF16))
        out_specs += [pl.BlockSpec(memory_space=pltpu.HBM), VMEM]
    width = JOIN * TILE
    scratch = [pltpu.VMEM(((len(hops) * chunks + 1) * TILE, TILE), BF16)]
    scratch += [pltpu.VMEM((slots, TILE), F32)] * 3
    scratch += [pltpu.SMEM((slots + JOIN,), jnp.int32), pltpu.VMEM((width, TILE), BF16)]
    scratch += [pltpu.VMEM((n, width), F32) for n in (GX, HALF, HALF, levels)]
    scratch += [pltpu.VMEM((HALF, levels, width), F32)] * 2
    if last:
        scratch += [pltpu.VMEM((G_OWN, half, TILE), F32), pltpu.SemaphoreType.DMA((GX,))]
    return pl.pallas_call(
        functools.partial(main_kernel, hops=hops, capacity=capacity, first=first, last=last),
        out_shape=out_shape,
        in_specs=[VMEM] * len(operands),
        out_specs=out_specs,
        scratch_shapes=scratch,
        input_output_aliases=aliases,
        compiler_params=PARAMS,
    )(*operands)


def finish_kernel(partial, other, out, total, sems):
    upper = (1 - lax.axis_index("sect")) * HALF
    copies = []
    for j in range(G_OWN):
        total[j] = other[j].astype(F32)
        if j % HALF == HALF - 1:
            for i in range(j + 1 - HALF, j + 1):
                column = (i // HALF) * GY + upper + i % HALF
                copies.append(
                    pltpu.make_async_copy(total.at[i], out.at[:, column, :], sems.at[i // HALF])
                )
                copies[-1].start()
    for copy in copies:
        copy.wait()


def shards(
    obs_weight,
    obs_frac,
    obs_cell,
    obs_level,
    obs_count,
    reach,
    length_x,
    length_y,
    tilt,
    vert_len,
    balance,
):
    levels = balance.shape[0]
    capacity = obs_weight.shape[2]
    blocks = lax.axis_size("blk")
    scales = [v.reshape(1, levels) for v in (length_x, length_y, tilt, vert_len)]
    packet, scale, left = pack(
        obs_count, reach, obs_weight, obs_frac, obs_cell, obs_level, scales, balance
    )

    def move(value, where):
        return lax.ppermute(value, "blk", [(i, where(i) % blocks) for i in range(blocks)])

    def swap(i):
        return i + 1 if i % 2 == 0 else i - 1

    def mate(value):
        return lax.ppermute(value, "sect", [(0, 1), (1, 0)])

    def both(values):
        return tuple(v for value in values for v in (value, mate(value)))

    def twice(hops):
        return tuple(hop for hop in hops for _ in range(2))

    cross = move(packet, lambda i: i - 3 if i % 2 == 0 else i + 3)
    up = move(packet, lambda i: i + 2)
    down = move(packet, lambda i: i - 2)
    near = move(packet, swap)
    (acc,) = main_call(scale, None, both((packet,)), twice(((0, 0),)), capacity)
    up, down, acc = lax.optimization_barrier((up, down, acc))
    near_up = move(up, swap)
    near_down = move(down, swap)
    (acc,) = main_call(
        scale, acc, both((up, down, near)), twice(((2, 2), (-2, -2), (-1, 1))), capacity
    )
    cross, near_up, near_down, acc = lax.optimization_barrier((cross, near_up, near_down, acc))
    _, partial, other = main_call(
        scale, acc, both((cross, near_up, near_down)), twice(((3, -3), (1, 3), (-3, -1))), capacity, left
    )
    half = levels // 2
    return pl.pallas_call(
        finish_kernel,
        out_shape=jax.ShapeDtypeStruct((half, G_DEV, TILE), F32),
        in_specs=[pl.BlockSpec(memory_space=pltpu.HBM), VMEM],
        out_specs=pl.BlockSpec(memory_space=pltpu.HBM),
        scratch_shapes=[pltpu.VMEM((G_OWN, half, TILE), F32), pltpu.SemaphoreType.DMA((GX,))],
        input_output_aliases={0: 0},
        compiler_params=PARAMS,
    )(partial, mate(other))


def solution(mesh):
    placed = (
        P(("date", "blk"), "sect", None, None),
        P(("date", "blk"), "sect", None, None),
        P(("date", "blk"), "sect", None),
        P(("date", "blk"), "sect", None),
        P(("date", "blk"), "sect"),
        P(("date", "blk"), None),
        P(),
        P(),
        P(),
        P(),
        P(),
    )
    return jax.shard_map(
        shards,
        mesh=mesh,
        in_specs=placed,
        out_specs=P("sect", ("date", "blk"), None),
        check_vma=False,
    )
```

```python
import functools
import jax
import jax.numpy as jnp
from jax import lax
from jax.experimental import pallas as pl
from jax.experimental.pallas import tpu as pltpu
from jax.sharding import PartitionSpec as P

GX = 8
GY = 16
G_DEV = GX * GY
TILE = 128
HALF = GY // 2
G_OWN = GX * HALF
JOIN = 2
GROUP = 16
F32 = jnp.float32
BF16 = jnp.bfloat16
VMEM = pl.BlockSpec(memory_space=pltpu.VMEM)
SMEM = pl.BlockSpec(memory_space=pltpu.SMEM)
PARAMS = pltpu.CompilerParams(vmem_limit_bytes=20 << 20)


def pack_kernel(
    count_ref,
    reach_hbm,
    weight_hbm,
    frac_hbm,
    cell_hbm,
    level_hbm,
    lx_hbm,
    ly_hbm,
    tl_hbm,
    vl_hbm,
    balance_hbm,
    out_ref,
    scale_ref,
    left_ref,
    reach_ref,
    weight_ref,
    frac_ref,
    cell_ref,
    level_ref,
    lx_ref,
    ly_ref,
    tl_ref,
    vl_ref,
    balance_ref,
    sems,
):
    pairs = (
        (weight_hbm, weight_ref),
        (frac_hbm, frac_ref),
        (cell_hbm, cell_ref),
        (level_hbm, level_ref),
        (reach_hbm, reach_ref),
        (lx_hbm, lx_ref),
        (ly_hbm, ly_ref),
        (tl_hbm, tl_ref),
        (vl_hbm, vl_ref),
        (balance_hbm, balance_ref),
    )
    copies = [pltpu.make_async_copy(src, dst, sems.at[i]) for i, (src, dst) in enumerate(pairs)]
    for copy in copies:
        copy.start()
    for copy in copies:
        copy.wait()
    capacity = weight_ref.shape[2]
    chunks = capacity // TILE
    levels = lx_ref.shape[1]
    half = levels // 2
    count = count_ref[0, 0]
    row = lax.broadcasted_iota(jnp.int32, (capacity, TILE), 0)
    weight = weight_ref[0, 0].astype(F32)
    out_ref[0:capacity, :] = jnp.where(row < count, weight, 0.0).astype(BF16)
    fraction = frac_ref[0, 0].astype(F32)
    cell = cell_ref[0].astype(F32)
    level = level_ref[0].astype(F32)
    rows = []
    for table in (fraction[0:1], fraction[1:2], cell, level):
        for i in range(chunks):
            rows.append(table[:, i * TILE : (i + 1) * TILE])
    out_ref[capacity : capacity + 4 * chunks, :] = jnp.concatenate(rows, 0).astype(BF16)
    live = (count + TILE - 1) // TILE
    code = live + 8 * (reach_ref[0, 0] + 4 * reach_ref[0, 1])
    tail = out_ref.shape[0] - capacity - 4 * chunks
    out_ref[capacity + 4 * chunks :, :] = jnp.full((tail, TILE), code, jnp.int32).astype(F32).astype(BF16)
    inv_x = 1.0 / lx_ref[...]
    inv_y = 1.0 / ly_ref[...]
    tilt = tl_ref[...]
    lines = [inv_x, tilt * inv_y, (1.0 - tilt * tilt) * inv_y * inv_y, 1.0 / vl_ref[...]]
    scale_ref[...] = jnp.transpose(jnp.concatenate(lines + lines, 0))
    mine = lax.axis_index("sect")
    matrix = jnp.concatenate(
        [
            balance_ref[pl.ds(pl.multiple_of(mine * half, half), half), :],
            balance_ref[pl.ds(pl.multiple_of((1 - mine) * half, half), half), :],
        ],
        0,
    )
    high = matrix.astype(BF16)
    low = (matrix - high.astype(F32)).astype(BF16)
    left_ref[...] = jnp.concatenate([high, low, high], 1)


def pack(obs_count, reach, obs_weight, obs_frac, obs_cell, obs_level, scales, balance):
    capacity = obs_weight.shape[2]
    levels = balance.shape[0]
    rows = capacity + 4 * (capacity // TILE) + 16
    operands = [obs_count, reach, obs_weight, obs_frac, obs_cell, obs_level, *scales, balance]
    operands[1:] = [pltpu.with_memory_space_constraint(v, pltpu.HBM) for v in operands[1:]]
    spaces = [pltpu.SMEM] + [pltpu.VMEM] * 9
    return pl.pallas_call(
        pack_kernel,
        out_shape=(
            jax.ShapeDtypeStruct((rows, TILE), BF16),
            jax.ShapeDtypeStruct((levels, 8), F32),
            jax.ShapeDtypeStruct((levels, 3 * levels), BF16),
        ),
        in_specs=[SMEM] + [pl.BlockSpec(memory_space=pltpu.HBM)] * (len(operands) - 1),
        out_specs=(VMEM, VMEM, VMEM),
        scratch_shapes=[space(v.shape, v.dtype) for space, v in zip(spaces, operands[1:])]
        + [pltpu.SemaphoreType.DMA((len(operands) - 1,))],
        compiler_params=PARAMS,
    )(*operands)


def gather_chunks(packets, offsets, capacity, w_all, ox_all, oy_all, le_all, order):
    chunks = capacity // TILE
    filled = jnp.int32(0)
    for i, (packet, offset) in enumerate(zip(packets, offsets)):
        w_all[i * capacity : (i + 1) * capacity, :] = packet[0:capacity, :]
        place = packet[capacity : capacity + 4 * chunks, :].astype(F32)
        fx, fy, cell, level = (place[t * chunks : (t + 1) * chunks] for t in range(4))
        cx = jnp.floor(cell * (1.0 / GY))
        cy = cell - cx * GY
        shift = jnp.full((1, TILE), offset, jnp.int32).astype(F32)
        ox_all[i * chunks : (i + 1) * chunks, :] = (cx + fx) * (1.0 / GX) - shift
        oy_all[i * chunks : (i + 1) * chunks, :] = (cy + fy) * (1.0 / GY)
        le_all[i * chunks : (i + 1) * chunks, :] = level
        tail = packet[capacity + 4 * chunks :, :].astype(F32)
        code = jnp.max(tail).astype(jnp.int32)
        live = code & 7
        below = (code >> 3) & 3
        above = (code >> 5) & 3
        used = jnp.where((offset <= above) & (-offset <= below), live, 0)
        for c in range(chunks):
            order[filled + c] = i * chunks + c
        filled = filled + used
    blank = len(packets) * chunks
    w_all[blank * TILE : (blank + 1) * TILE, :] = jnp.zeros((TILE, TILE), BF16)
    for ref in (ox_all, oy_all, le_all):
        ref[blank : blank + 8, :] = jnp.zeros((8, TILE), F32)
    for c in range(JOIN - 1):
        order[filled + c] = blank
    return filled


def spread(filled, scale, acc, w_all, ox_all, oy_all, le_all, order, wq, dxs, dys, dzs, sx, ys, zs):
    levels = scale.shape[0]
    inv_x = scale[:, 0:1]
    tilt_y = scale[:, 1:2]
    rest_y = scale[:, 2:3]
    inv_v = scale[:, 3:4]
    height = lax.broadcasted_iota(jnp.int32, (levels, 1), 0).astype(F32)
    grid_x = (lax.broadcasted_iota(jnp.int32, (GX, 1), 0).astype(F32) + 0.5) / GX
    lower = lax.axis_index("sect") * HALF
    grid_y = ((lax.broadcasted_iota(jnp.int32, (HALF, 1), 0) + lower).astype(F32) + 0.5) / GY

    def join(q, _):
        picks = [order[q * JOIN + i] for i in range(JOIN)]
        for i, r in enumerate(picks):
            wq[i * TILE : (i + 1) * TILE, :] = w_all[pl.ds(pl.multiple_of(r * TILE, TILE), TILE), :]

        def lanes(ref):
            return jnp.concatenate([ref[pl.ds(r, 1), :] for r in picks], 1)

        dxs[...] = grid_x - lanes(ox_all)
        dy = grid_y - lanes(oy_all)
        dys[...] = dy
        dzs[...] = dy * dy
        sep = (height - lanes(le_all)) * inv_v
        root = lax.rsqrt(lax.rsqrt(1.0 + sep * sep))
        full = root * root
        sx[...] = root * inv_x
        sy = root * tilt_y
        sz = full * rest_y
        for i in range(HALF):
            ys[i] = sy * dys[i : i + 1, :]
            zs[i] = sz * dzs[i : i + 1, :] + full
        right = wq[...]
        for first in range(0, levels, GROUP):
            span = slice(first, first + GROUP)
            rows = []
            for i in range(GX):
                xv = sx[span, :] * dxs[i : i + 1, :]
                for j in range(HALF):
                    a = xv + ys[j, span, :]
                    y = a * a + zs[j, span, :]
                    rows.append((1.0 / (y * y)).astype(BF16))
            term = jnp.dot(jnp.concatenate(rows, 0), right, preferred_element_type=F32)
            for j in range(G_OWN):
                at = slice(j * levels + first, j * levels + first + GROUP)
                acc[at, :] += term[j * GROUP : (j + 1) * GROUP]
        return 0

    lax.fori_loop(0, (filled + JOIN - 1) // JOIN, join, 0)


def balance_step(left_ref, acc, out, other, own, sems):
    levels = left_ref.shape[0]
    half = levels // 2
    left = left_ref[...]
    lower = lax.axis_index("sect") * HALF
    copies = []
    for j in range(0, G_OWN, 2):
        value = jnp.concatenate([acc[(j + n) * levels : (j + n + 1) * levels, :] for n in range(2)], 1)
        big = value.astype(BF16)
        small = (value - big.astype(F32)).astype(BF16)
        right = jnp.concatenate([big, big, small], 0)
        result = jnp.dot(left, right, preferred_element_type=F32)
        for n in range(2):
            own[j + n] = result[0:half, n * TILE : (n + 1) * TILE]
            other[j + n] = result[half:, n * TILE : (n + 1) * TILE].astype(BF16)
    for j in range(G_OWN):
        column = (j // HALF) * GY + lower + j % HALF
        copies.append(pltpu.make_async_copy(own.at[j], out.at[:, column, :], sems.at[j // HALF]))
        copies[-1].start()
    for copy in copies:
        copy.wait()


def main_kernel(*refs, hops, capacity, first, last):
    refs = list(refs)
    scale = refs.pop(0)
    if not first:
        refs.pop(0)
    groups = refs[:2]
    refs = refs[2:]
    rows = capacity + 4 * (capacity // TILE) + 16
    packets = [group.at[i * rows : (i + 1) * rows, :] for group in groups for i in range(len(hops) // 2)]
    left = refs.pop(0) if last else None
    acc = refs.pop(0)
    if last:
        out, other = refs[:2]
        own, sems = refs[-2:]
        refs = refs[2:-2]
    if first:
        acc[...] = jnp.zeros(acc.shape, F32)
    parity = lax.rem(lax.axis_index("blk"), 2)
    offsets = [even if even == odd else jnp.where(parity == 0, even, odd) for even, odd in hops]
    filled = gather_chunks(packets, offsets, capacity, *refs[:5])
    spread(filled, scale, acc, *refs)
    if last:
        balance_step(left, acc, out, other, own, sems)


def main_call(scale, acc, packets, hops, capacity, left=None):
    first = acc is None
    last = left is not None
    levels = scale.shape[0]
    chunks = capacity // TILE
    slots = len(hops) * chunks + 8
    operands = [scale]
    aliases = {}
    if not first:
        aliases = {1: 0}
        operands.append(acc)
    operands += list(packets)
    out_shape = [jax.ShapeDtypeStruct((levels * G_OWN, TILE), F32)]
    out_specs = [VMEM]
    if last:
        operands.append(left)
        half = levels // 2
        out_shape.append(jax.ShapeDtypeStruct((half, G_DEV, TILE), F32))
        out_shape.append(jax.ShapeDtypeStruct((G_OWN, half, TILE), BF16))
        out_specs += [pl.BlockSpec(memory_space=pltpu.HBM), VMEM]
    width = JOIN * TILE
    scratch = [pltpu.VMEM(((len(hops) * chunks + 1) * TILE, TILE), BF16)]
    scratch += [pltpu.VMEM((slots, TILE), F32)] * 3
    scratch += [pltpu.SMEM((slots + JOIN,), jnp.int32), pltpu.VMEM((width, TILE), BF16)]
    scratch += [pltpu.VMEM((n, width), F32) for n in (GX, HALF, HALF, levels)]
    scratch += [pltpu.VMEM((HALF, levels, width), F32)] * 2
    if last:
        scratch += [pltpu.VMEM((G_OWN, half, TILE), F32), pltpu.SemaphoreType.DMA((GX,))]
    return pl.pallas_call(
        functools.partial(main_kernel, hops=hops, capacity=capacity, first=first, last=last),
        out_shape=out_shape,
        in_specs=[VMEM] * len(operands),
        out_specs=out_specs,
        scratch_shapes=scratch,
        input_output_aliases=aliases,
        compiler_params=PARAMS,
    )(*operands)


def finish_kernel(partial, other, out, total, sems):
    upper = (1 - lax.axis_index("sect")) * HALF
    copies = []
    for j in range(G_OWN):
        total[j] = other[j].astype(F32)
        if j % HALF == HALF - 1:
            for i in range(j + 1 - HALF, j + 1):
                column = (i // HALF) * GY + upper + i % HALF
                copies.append(
                    pltpu.make_async_copy(total.at[i], out.at[:, column, :], sems.at[i // HALF])
                )
                copies[-1].start()
    for copy in copies:
        copy.wait()


def shards(
    obs_weight,
    obs_frac,
    obs_cell,
    obs_level,
    obs_count,
    reach,
    length_x,
    length_y,
    tilt,
    vert_len,
    balance,
):
    levels = balance.shape[0]
    capacity = obs_weight.shape[2]
    blocks = lax.axis_size("blk")
    scales = [v.reshape(1, levels) for v in (length_x, length_y, tilt, vert_len)]
    packet, scale, left = pack(
        obs_count, reach, obs_weight, obs_frac, obs_cell, obs_level, scales, balance
    )

    def move(value, where):
        return lax.ppermute(value, "blk", [(i, where(i) % blocks) for i in range(blocks)])

    def swap(i):
        return i + 1 if i % 2 == 0 else i - 1

    def mate(value):
        return lax.ppermute(value, "sect", [(0, 1), (1, 0)])

    other_own = mate(packet)
    up = move(packet, lambda i: i + 2)
    down = move(packet, lambda i: i - 2)
    near = move(packet, swap)
    cross = move(packet, lambda i: i - 3 if i % 2 == 0 else i + 3)
    (acc,) = main_call(scale, None, (packet, other_own), ((0, 0),) * 2, capacity)
    up, down, acc = lax.optimization_barrier((up, down, acc))
    near_up = move(up, swap)
    near_down = move(down, swap)
    middle = jnp.concatenate([up, down, near], 0)
    other_middle = mate(middle)
    (acc,) = main_call(
        scale, acc, (middle, other_middle), ((2, 2), (-2, -2), (-1, 1)) * 2, capacity
    )
    cross, near_up, near_down, acc = lax.optimization_barrier((cross, near_up, near_down, acc))
    final = jnp.concatenate([cross, near_up, near_down], 0)
    other_final = mate(final)
    _, partial, other = main_call(
        scale, acc, (final, other_final), ((3, -3), (1, 3), (-3, -1)) * 2, capacity, left
    )
    half = levels // 2
    return pl.pallas_call(
        finish_kernel,
        out_shape=jax.ShapeDtypeStruct((half, G_DEV, TILE), F32),
        in_specs=[pl.BlockSpec(memory_space=pltpu.HBM), VMEM],
        out_specs=pl.BlockSpec(memory_space=pltpu.HBM),
        scratch_shapes=[pltpu.VMEM((G_OWN, half, TILE), F32), pltpu.SemaphoreType.DMA((GX,))],
        input_output_aliases={0: 0},
        compiler_params=PARAMS,
    )(partial, mate(other))


def solution(mesh):
    placed = (
        P(("date", "blk"), "sect", None, None),
        P(("date", "blk"), "sect", None, None),
        P(("date", "blk"), "sect", None),
        P(("date", "blk"), "sect", None),
        P(("date", "blk"), "sect"),
        P(("date", "blk"), None),
        P(),
        P(),
        P(),
        P(),
        P(),
    )
    return jax.shard_map(
        shards,
        mesh=mesh,
        in_specs=placed,
        out_specs=P("sect", ("date", "blk"), None),
        check_vma=False,
    )
```

```python
import functools
import jax
import jax.numpy as jnp
from jax import lax
from jax.experimental import pallas as pl
from jax.experimental.pallas import tpu as pltpu
from jax.sharding import PartitionSpec as P

GX = 8
GY = 16
G_DEV = GX * GY
TILE = 128
JOIN = 2
GROUP = 16
F32 = jnp.float32
BF16 = jnp.bfloat16
VMEM = pl.BlockSpec(memory_space=pltpu.VMEM)
SMEM = pl.BlockSpec(memory_space=pltpu.SMEM)
PARAMS = pltpu.CompilerParams(vmem_limit_bytes=20 << 20)


def pack_kernel(
    count_ref,
    reach_hbm,
    weight_hbm,
    frac_hbm,
    cell_hbm,
    level_hbm,
    lx_hbm,
    ly_hbm,
    tl_hbm,
    vl_hbm,
    balance_hbm,
    out_ref,
    scale_ref,
    left_ref,
    reach_ref,
    weight_ref,
    frac_ref,
    cell_ref,
    level_ref,
    lx_ref,
    ly_ref,
    tl_ref,
    vl_ref,
    balance_ref,
    sems,
):
    pairs = (
        (weight_hbm, weight_ref),
        (frac_hbm, frac_ref),
        (cell_hbm, cell_ref),
        (level_hbm, level_ref),
        (reach_hbm, reach_ref),
        (lx_hbm, lx_ref),
        (ly_hbm, ly_ref),
        (tl_hbm, tl_ref),
        (vl_hbm, vl_ref),
        (balance_hbm, balance_ref),
    )
    copies = [pltpu.make_async_copy(src, dst, sems.at[i]) for i, (src, dst) in enumerate(pairs)]
    for copy in copies:
        copy.start()
    for copy in copies:
        copy.wait()
    capacity = weight_ref.shape[2]
    chunks = capacity // TILE
    levels = lx_ref.shape[1]
    half = levels // 2
    count = count_ref[0, 0]
    row = lax.broadcasted_iota(jnp.int32, (capacity, TILE), 0)
    weight = weight_ref[0, 0].astype(F32)
    out_ref[0:capacity, :] = jnp.where(row < count, weight, 0.0).astype(BF16)
    fraction = frac_ref[0, 0].astype(F32)
    cell = cell_ref[0].astype(F32)
    level = level_ref[0].astype(F32)
    rows = []
    for table in (fraction[0:1], fraction[1:2], cell, level):
        for i in range(chunks):
            rows.append(table[:, i * TILE : (i + 1) * TILE])
    out_ref[capacity : capacity + 4 * chunks, :] = jnp.concatenate(rows, 0).astype(BF16)
    live = (count + TILE - 1) // TILE
    code = live + 8 * (reach_ref[0, 0] + 4 * reach_ref[0, 1])
    tail = out_ref.shape[0] - capacity - 4 * chunks
    out_ref[capacity + 4 * chunks :, :] = jnp.full((tail, TILE), code, jnp.int32).astype(F32).astype(BF16)
    inv_x = 1.0 / lx_ref[...]
    inv_y = 1.0 / ly_ref[...]
    tilt = tl_ref[...]
    lines = [inv_x, tilt * inv_y, (1.0 - tilt * tilt) * inv_y * inv_y, 1.0 / vl_ref[...]]
    scale_ref[...] = jnp.transpose(jnp.concatenate(lines + lines, 0))
    mine = lax.axis_index("sect")
    matrix = jnp.concatenate(
        [
            balance_ref[pl.ds(pl.multiple_of(mine * half, half), half), :],
            balance_ref[pl.ds(pl.multiple_of((1 - mine) * half, half), half), :],
        ],
        0,
    )
    high = matrix.astype(BF16)
    low = (matrix - high.astype(F32)).astype(BF16)
    left_ref[...] = jnp.concatenate([high, low, high], 1)


def pack(obs_count, reach, obs_weight, obs_frac, obs_cell, obs_level, scales, balance):
    capacity = obs_weight.shape[2]
    levels = balance.shape[0]
    rows = capacity + 4 * (capacity // TILE) + 16
    operands = [obs_count, reach, obs_weight, obs_frac, obs_cell, obs_level, *scales, balance]
    operands[1:] = [pltpu.with_memory_space_constraint(v, pltpu.HBM) for v in operands[1:]]
    spaces = [pltpu.SMEM] + [pltpu.VMEM] * 9
    return pl.pallas_call(
        pack_kernel,
        out_shape=(
            jax.ShapeDtypeStruct((rows, TILE), BF16),
            jax.ShapeDtypeStruct((levels, 8), F32),
            jax.ShapeDtypeStruct((levels, 3 * levels), BF16),
        ),
        in_specs=[SMEM] + [pl.BlockSpec(memory_space=pltpu.HBM)] * (len(operands) - 1),
        out_specs=(VMEM, VMEM, VMEM),
        scratch_shapes=[space(v.shape, v.dtype) for space, v in zip(spaces, operands[1:])]
        + [pltpu.SemaphoreType.DMA((len(operands) - 1,))],
        compiler_params=PARAMS,
    )(*operands)


def gather_chunks(packets, offsets, capacity, w_all, ox_all, oy_all, le_all, order):
    chunks = capacity // TILE
    filled = jnp.int32(0)
    for i, (packet, offset) in enumerate(zip(packets, offsets)):
        w_all[i * capacity : (i + 1) * capacity, :] = packet[0:capacity, :]
        place = packet[capacity : capacity + 4 * chunks, :].astype(F32)
        fx, fy, cell, level = (place[t * chunks : (t + 1) * chunks] for t in range(4))
        cx = jnp.floor(cell * (1.0 / GY))
        cy = cell - cx * GY
        shift = jnp.full((1, TILE), offset, jnp.int32).astype(F32)
        ox_all[i * chunks : (i + 1) * chunks, :] = (cx + fx) * (1.0 / GX) - shift
        oy_all[i * chunks : (i + 1) * chunks, :] = (cy + fy) * (1.0 / GY)
        le_all[i * chunks : (i + 1) * chunks, :] = level
        tail = packet[capacity + 4 * chunks :, :].astype(F32)
        code = jnp.max(tail).astype(jnp.int32)
        live = code & 7
        below = (code >> 3) & 3
        above = (code >> 5) & 3
        used = jnp.where((offset <= above) & (-offset <= below), live, 0)
        for c in range(chunks):
            order[filled + c] = i * chunks + c
        filled = filled + used
    blank = len(packets) * chunks
    w_all[blank * TILE : (blank + 1) * TILE, :] = jnp.zeros((TILE, TILE), BF16)
    for ref in (ox_all, oy_all, le_all):
        ref[blank : blank + 8, :] = jnp.zeros((8, TILE), F32)
    for c in range(JOIN - 1):
        order[filled + c] = blank
    return filled


def spread(filled, scale, acc, w_all, ox_all, oy_all, le_all, order, wq, dxs, dys, dzs, sx, ys, zs):
    levels = scale.shape[0]
    inv_x = scale[:, 0:1]
    tilt_y = scale[:, 1:2]
    rest_y = scale[:, 2:3]
    inv_v = scale[:, 3:4]
    height = lax.broadcasted_iota(jnp.int32, (levels, 1), 0).astype(F32)
    grid_x = (lax.broadcasted_iota(jnp.int32, (GX, 1), 0).astype(F32) + 0.5) / GX
    grid_y = (lax.broadcasted_iota(jnp.int32, (GY, 1), 0).astype(F32) + 0.5) / GY

    def join(q, _):
        picks = [order[q * JOIN + i] for i in range(JOIN)]
        for i, r in enumerate(picks):
            wq[i * TILE : (i + 1) * TILE, :] = w_all[pl.ds(pl.multiple_of(r * TILE, TILE), TILE), :]

        def lanes(ref):
            return jnp.concatenate([ref[pl.ds(r, 1), :] for r in picks], 1)

        dxs[...] = grid_x - lanes(ox_all)
        dy = grid_y - lanes(oy_all)
        dys[...] = dy
        dzs[...] = dy * dy
        sep = (height - lanes(le_all)) * inv_v
        root = lax.rsqrt(lax.rsqrt(1.0 + sep * sep))
        full = root * root
        sx[...] = root * inv_x
        sy_all = root * tilt_y
        sz_all = full * rest_y
        right = wq[...]
        for first in range(0, levels, GROUP):
            span = slice(first, first + GROUP)
            for i in range(GY):
                ys[i, span, :] = sy_all[span] * dys[i : i + 1, :]
                zs[i, span, :] = sz_all[span] * dzs[i : i + 1, :] + full[span]
            rows = []
            for i in range(GX):
                xv = sx[span, :] * dxs[i : i + 1, :]
                for j in range(GY):
                    a = xv + ys[j, span, :]
                    y = a * a + zs[j, span, :]
                    rows.append((1.0 / (y * y)).astype(BF16))
            term = jnp.dot(jnp.concatenate(rows, 0), right, preferred_element_type=F32)
            for j in range(G_DEV):
                at = slice(j * levels + first, j * levels + first + GROUP)
                acc[at, :] += term[j * GROUP : (j + 1) * GROUP]
        return 0

    lax.fori_loop(0, (filled + JOIN - 1) // JOIN, join, 0)


def balance_step(left_ref, acc, own, other, base):
    levels = left_ref.shape[0]
    half = levels // 2
    left = left_ref[...]
    for j in range(0, own.shape[0], 2):
        value = jnp.concatenate(
            [acc[(base + j + n) * levels : (base + j + n + 1) * levels, :] for n in range(2)], 1
        )
        big = value.astype(BF16)
        small = (value - big.astype(F32)).astype(BF16)
        right = jnp.concatenate([big, big, small], 0)
        result = jnp.dot(left, right, preferred_element_type=F32)
        for n in range(2):
            own[j + n] = result[0:half, n * TILE : (n + 1) * TILE]
            other[j + n] = result[half:, n * TILE : (n + 1) * TILE].astype(BF16)


def rest_kernel(left, acc, own, other):
    balance_step(left, acc, own, other, G_DEV // 2)


def main_kernel(*refs, hops, capacity, first, last):
    refs = list(refs)
    scale = refs.pop(0)
    if not first:
        refs.pop(0)
    rows = capacity + 4 * (capacity // TILE) + 16
    packets = []
    while len(packets) < len(hops):
        group = refs.pop(0)
        for i in range(group.shape[0] // rows):
            packets.append(group.at[i * rows : (i + 1) * rows, :])
    left = refs.pop(0) if last else None
    acc = refs.pop(0)
    if last:
        own, other = refs[:2]
        refs = refs[2:]
    if first:
        acc[...] = jnp.zeros(acc.shape, F32)
    parity = lax.rem(lax.axis_index("blk"), 2)
    offsets = [even if even == odd else jnp.where(parity == 0, even, odd) for even, odd in hops]
    filled = gather_chunks(packets, offsets, capacity, *refs[:5])
    spread(filled, scale, acc, *refs)
    if last:
        balance_step(left, acc, own, other, 0)


def main_call(scale, acc, packets, hops, capacity, left=None):
    first = acc is None
    last = left is not None
    levels = scale.shape[0]
    chunks = capacity // TILE
    slots = len(hops) * chunks + 8
    operands = [scale]
    aliases = {}
    if not first:
        aliases = {1: 0}
        operands.append(acc)
    operands += list(packets)
    out_shape = [jax.ShapeDtypeStruct((levels * G_DEV, TILE), F32)]
    if last:
        operands.append(left)
        half = levels // 2
        out_shape.append(jax.ShapeDtypeStruct((G_DEV // 2, half, TILE), F32))
        out_shape.append(jax.ShapeDtypeStruct((G_DEV // 2, half, TILE), BF16))
    width = JOIN * TILE
    scratch = [pltpu.VMEM(((len(hops) * chunks + 1) * TILE, TILE), BF16)]
    scratch += [pltpu.VMEM((slots, TILE), F32)] * 3
    scratch += [pltpu.SMEM((slots + JOIN,), jnp.int32), pltpu.VMEM((width, TILE), BF16)]
    scratch += [pltpu.VMEM((n, width), F32) for n in (GX, GY, GY, levels)]
    scratch += [pltpu.VMEM((GY, levels, width), F32)] * 2
    return pl.pallas_call(
        functools.partial(main_kernel, hops=hops, capacity=capacity, first=first, last=last),
        out_shape=out_shape,
        in_specs=[VMEM] * len(operands),
        out_specs=[VMEM] * len(out_shape),
        scratch_shapes=scratch,
        input_output_aliases=aliases,
        compiler_params=PARAMS,
    )(*operands)


def finish_kernel(*refs, base):
    own, other = refs[:2]
    out, total, sems = refs[-3:]
    parts = sems.shape[0]
    count = own.shape[0]
    width = count // parts
    copies = []
    for p in range(parts):
        for j in range(p * width, (p + 1) * width):
            total[j] = own[j] + other[j].astype(F32)
        for j in range(p * width, (p + 1) * width):
            copies.append(pltpu.make_async_copy(total.at[j], out.at[:, base + j, :], sems.at[p]))
            copies[-1].start()
    for copy in copies:
        copy.wait()


def finish(own, other, out, base):
    count, half, width = own.shape
    operands = [own, other]
    specs = [VMEM, VMEM]
    aliases = {}
    if out is not None:
        operands.append(out)
        specs.append(pl.BlockSpec(memory_space=pltpu.HBM))
        aliases = {2: 0}
    return pl.pallas_call(
        functools.partial(finish_kernel, base=base),
        out_shape=jax.ShapeDtypeStruct((half, G_DEV, width), F32),
        in_specs=specs,
        out_specs=pl.BlockSpec(memory_space=pltpu.HBM),
        scratch_shapes=[pltpu.VMEM((count, half, width), F32), pltpu.SemaphoreType.DMA((4,))],
        input_output_aliases=aliases,
        compiler_params=PARAMS,
    )(*operands)


def shards(
    obs_weight,
    obs_frac,
    obs_cell,
    obs_level,
    obs_count,
    reach,
    length_x,
    length_y,
    tilt,
    vert_len,
    balance,
):
    levels = balance.shape[0]
    capacity = obs_weight.shape[2]
    blocks = lax.axis_size("blk")
    scales = [v.reshape(1, levels) for v in (length_x, length_y, tilt, vert_len)]
    packet, scale, left = pack(
        obs_count, reach, obs_weight, obs_frac, obs_cell, obs_level, scales, balance
    )

    def move(value, where):
        return lax.ppermute(value, "blk", [(i, where(i) % blocks) for i in range(blocks)])

    def swap(i):
        return i + 1 if i % 2 == 0 else i - 1

    up = move(packet, lambda i: i + 2)
    down = move(packet, lambda i: i - 2)
    near = move(packet, swap)
    cross = move(packet, lambda i: i - 3 if i % 2 == 0 else i + 3)
    (acc,) = main_call(scale, None, (packet,), ((0, 0),), capacity)
    up, down, acc = lax.optimization_barrier((up, down, acc))
    sides = jnp.concatenate([up, down], 0)
    near_sides = move(sides, swap)
    (acc,) = main_call(scale, acc, (sides, near), ((2, 2), (-2, -2), (-1, 1)), capacity)
    cross, acc = lax.optimization_barrier((cross, acc))
    (acc,) = main_call(scale, acc, (cross,), ((3, -3),), capacity)
    near_sides, acc = lax.optimization_barrier((near_sides, acc))
    acc, own, other = main_call(scale, acc, (near_sides,), ((1, 3), (-3, -1)), capacity, left)
    half = levels // 2
    first_other = lax.ppermute(other, "sect", [(0, 1), (1, 0)])
    rest_own, rest_other = pl.pallas_call(
        rest_kernel,
        out_shape=(
            jax.ShapeDtypeStruct((G_DEV // 2, half, TILE), F32),
            jax.ShapeDtypeStruct((G_DEV // 2, half, TILE), BF16),
        ),
        in_specs=[VMEM, VMEM],
        out_specs=(VMEM, VMEM),
        compiler_params=PARAMS,
    )(left, acc)
    second_other = lax.ppermute(rest_other, "sect", [(0, 1), (1, 0)])
    out = finish(own, first_other, None, 0)
    out = finish(rest_own, second_other, out, G_DEV // 2)
    return out


def solution(mesh):
    placed = (
        P(("date", "blk"), "sect", None, None),
        P(("date", "blk"), "sect", None, None),
        P(("date", "blk"), "sect", None),
        P(("date", "blk"), "sect", None),
        P(("date", "blk"), "sect"),
        P(("date", "blk"), None),
        P(),
        P(),
        P(),
        P(),
        P(),
    )
    return jax.shard_map(
        shards,
        mesh=mesh,
        in_specs=placed,
        out_specs=P("sect", ("date", "blk"), None),
        check_vma=False,
    )
```

```python
import functools
import jax
import jax.numpy as jnp
from jax import lax
from jax.experimental import pallas as pl
from jax.experimental.pallas import tpu as pltpu
from jax.sharding import PartitionSpec as P

GX = 8
GY = 16
G_DEV = GX * GY
TILE = 128
JOIN = 2
GROUP = 16
BITS = 7
F32 = jnp.float32
BF16 = jnp.bfloat16
VMEM = pl.BlockSpec(memory_space=pltpu.VMEM)
SMEM = pl.BlockSpec(memory_space=pltpu.SMEM)
PARAMS = pltpu.CompilerParams(vmem_limit_bytes=20 << 20)


def pack_kernel(
    count_ref,
    reach_hbm,
    weight_hbm,
    frac_hbm,
    cell_hbm,
    level_hbm,
    lx_hbm,
    ly_hbm,
    tl_hbm,
    vl_hbm,
    balance_hbm,
    out_ref,
    scale_ref,
    left_ref,
    reach_ref,
    weight_ref,
    frac_ref,
    cell_ref,
    level_ref,
    lx_ref,
    ly_ref,
    tl_ref,
    vl_ref,
    balance_ref,
    sems,
):
    pairs = (
        (weight_hbm, weight_ref),
        (frac_hbm, frac_ref),
        (cell_hbm, cell_ref),
        (level_hbm, level_ref),
        (reach_hbm, reach_ref),
        (lx_hbm, lx_ref),
        (ly_hbm, ly_ref),
        (tl_hbm, tl_ref),
        (vl_hbm, vl_ref),
        (balance_hbm, balance_ref),
    )
    copies = [pltpu.make_async_copy(src, dst, sems.at[i]) for i, (src, dst) in enumerate(pairs)]
    for copy in copies:
        copy.start()
    for copy in copies:
        copy.wait()
    capacity = weight_ref.shape[2]
    chunks = capacity // TILE
    levels = lx_ref.shape[1]
    half = levels // 2
    count = count_ref[0, 0]
    row = lax.broadcasted_iota(jnp.int32, (capacity, TILE), 0)
    weight = weight_ref[0, 0].astype(F32)
    out_ref[0:capacity, :] = jnp.where(row < count, weight, 0.0).astype(BF16)
    fraction = frac_ref[0, 0].astype(F32)
    cell = cell_ref[0].astype(F32)
    level = level_ref[0].astype(F32)
    live = (count + TILE - 1) // TILE
    code = live + 8 * (reach_ref[0, 0] + 4 * reach_ref[0, 1])
    lane = lax.broadcasted_iota(jnp.int32, (1, capacity), 1)
    flag = jnp.where(lane < BITS, lax.shift_right_logical(code, jnp.minimum(lane, BITS)) & 1, 0)
    cell = cell + (G_DEV * flag).astype(F32)
    rows = []
    for table in (fraction[0:1], fraction[1:2], cell, level):
        for i in range(chunks):
            rows.append(table[:, i * TILE : (i + 1) * TILE])
    out_ref[capacity : capacity + 4 * chunks, :] = jnp.concatenate(rows, 0).astype(BF16)
    inv_x = 1.0 / lx_ref[...]
    inv_y = 1.0 / ly_ref[...]
    tilt = tl_ref[...]
    lines = [inv_x, tilt * inv_y, (1.0 - tilt * tilt) * inv_y * inv_y, 1.0 / vl_ref[...]]
    scale_ref[...] = jnp.transpose(jnp.concatenate(lines + lines, 0))
    mine = lax.axis_index("sect")
    matrix = jnp.concatenate(
        [
            balance_ref[pl.ds(pl.multiple_of(mine * half, half), half), :],
            balance_ref[pl.ds(pl.multiple_of((1 - mine) * half, half), half), :],
        ],
        0,
    )
    high = matrix.astype(BF16)
    low = (matrix - high.astype(F32)).astype(BF16)
    left_ref[...] = jnp.concatenate([high, low, high], 1)


def pack(obs_count, reach, obs_weight, obs_frac, obs_cell, obs_level, scales, balance):
    capacity = obs_weight.shape[2]
    levels = balance.shape[0]
    rows = capacity + 4 * (capacity // TILE)
    operands = [obs_count, reach, obs_weight, obs_frac, obs_cell, obs_level, *scales, balance]
    operands[1:] = [pltpu.with_memory_space_constraint(v, pltpu.HBM) for v in operands[1:]]
    spaces = [pltpu.SMEM] + [pltpu.VMEM] * 9
    return pl.pallas_call(
        pack_kernel,
        out_shape=(
            jax.ShapeDtypeStruct((rows, TILE), BF16),
            jax.ShapeDtypeStruct((levels, 8), F32),
            jax.ShapeDtypeStruct((levels, 3 * levels), BF16),
        ),
        in_specs=[SMEM] + [pl.BlockSpec(memory_space=pltpu.HBM)] * (len(operands) - 1),
        out_specs=(VMEM, VMEM, VMEM),
        scratch_shapes=[space(v.shape, v.dtype) for space, v in zip(spaces, operands[1:])]
        + [pltpu.SemaphoreType.DMA((len(operands) - 1,))],
        compiler_params=PARAMS,
    )(*operands)


def gather_chunks(packets, offsets, capacity, w_all, ox_all, oy_all, le_all, order):
    chunks = capacity // TILE
    filled = jnp.int32(0)
    for i, (packet, offset) in enumerate(zip(packets, offsets)):
        w_all[i * capacity : (i + 1) * capacity, :] = packet[0:capacity, :]
        place = packet[capacity : capacity + 4 * chunks, :].astype(F32)
        fx, fy, cell, level = (place[t * chunks : (t + 1) * chunks] for t in range(4))
        high = cell >= G_DEV
        cell = jnp.where(high, cell - G_DEV, cell)
        lane = lax.broadcasted_iota(jnp.int32, (chunks, TILE), 1)
        weight = lax.shift_left(jnp.int32(1), jnp.minimum(lane, BITS)).astype(F32)
        cx = jnp.floor(cell * (1.0 / GY))
        cy = cell - cx * GY
        shift = jnp.full((1, TILE), offset, jnp.int32).astype(F32)
        ox_all[i * chunks : (i + 1) * chunks, :] = (cx + fx) * (1.0 / GX) - shift
        oy_all[i * chunks : (i + 1) * chunks, :] = (cy + fy) * (1.0 / GY)
        le_all[i * chunks : (i + 1) * chunks, :] = level
        code = jnp.sum(jnp.where(high, weight, 0.0)).astype(jnp.int32)
        live = code & 7
        below = (code >> 3) & 3
        above = (code >> 5) & 3
        used = jnp.where((offset <= above) & (-offset <= below), live, 0)
        for c in range(chunks):
            order[filled + c] = i * chunks + c
        filled = filled + used
    blank = len(packets) * chunks
    w_all[blank * TILE : (blank + 1) * TILE, :] = jnp.zeros((TILE, TILE), BF16)
    for ref in (ox_all, oy_all, le_all):
        ref[blank : blank + 8, :] = jnp.zeros((8, TILE), F32)
    for c in range(JOIN - 1):
        order[filled + c] = blank
    return filled


def spread(filled, scale, acc, w_all, ox_all, oy_all, le_all, order, wq, dxs, dys, dzs, sx, ys, zs):
    levels = scale.shape[0]
    inv_x = scale[:, 0:1]
    tilt_y = scale[:, 1:2]
    rest_y = scale[:, 2:3]
    inv_v = scale[:, 3:4]
    height = lax.broadcasted_iota(jnp.int32, (levels, 1), 0).astype(F32)
    grid_x = (lax.broadcasted_iota(jnp.int32, (GX, 1), 0).astype(F32) + 0.5) / GX
    grid_y = (lax.broadcasted_iota(jnp.int32, (GY, 1), 0).astype(F32) + 0.5) / GY

    def join(q, _):
        picks = [order[q * JOIN + i] for i in range(JOIN)]
        for i, r in enumerate(picks):
            wq[i * TILE : (i + 1) * TILE, :] = w_all[pl.ds(pl.multiple_of(r * TILE, TILE), TILE), :]

        def lanes(ref):
            return jnp.concatenate([ref[pl.ds(r, 1), :] for r in picks], 1)

        dxs[...] = grid_x - lanes(ox_all)
        dy = grid_y - lanes(oy_all)
        dys[...] = dy
        dzs[...] = dy * dy
        sep = (height - lanes(le_all)) * inv_v
        root = lax.rsqrt(lax.rsqrt(1.0 + sep * sep))
        full = root * root
        sx[...] = root * inv_x
        sy_all = root * tilt_y
        sz_all = full * rest_y
        right = wq[...]
        for first in range(0, levels, GROUP):
            span = slice(first, first + GROUP)
            for i in range(GY):
                ys[i, span, :] = sy_all[span] * dys[i : i + 1, :]
                zs[i, span, :] = sz_all[span] * dzs[i : i + 1, :] + full[span]
            rows = []
            for i in range(GX):
                xv = sx[span, :] * dxs[i : i + 1, :]
                for j in range(GY):
                    a = xv + ys[j, span, :]
                    y = a * a + zs[j, span, :]
                    rows.append((1.0 / (y * y)).astype(BF16))
            term = jnp.dot(jnp.concatenate(rows, 0), right, preferred_element_type=F32)
            for j in range(G_DEV):
                at = slice(j * levels + first, j * levels + first + GROUP)
                acc[at, :] += term[j * GROUP : (j + 1) * GROUP]
        return 0

    lax.fori_loop(0, (filled + JOIN - 1) // JOIN, join, 0)


def balance_step(left_ref, acc, own, other, base):
    levels = left_ref.shape[0]
    half = levels // 2
    left = left_ref[...]
    for j in range(0, own.shape[0], 2):
        value = jnp.concatenate(
            [acc[(base + j + n) * levels : (base + j + n + 1) * levels, :] for n in range(2)], 1
        )
        big = value.astype(BF16)
        small = (value - big.astype(F32)).astype(BF16)
        right = jnp.concatenate([big, big, small], 0)
        result = jnp.dot(left, right, preferred_element_type=F32)
        for n in range(2):
            own[j + n] = result[0:half, n * TILE : (n + 1) * TILE]
            other[j + n] = result[half:, n * TILE : (n + 1) * TILE].astype(BF16)


def rest_kernel(left, acc, own, other):
    balance_step(left, acc, own, other, G_DEV // 2)


def main_kernel(*refs, hops, capacity, first, last):
    refs = list(refs)
    scale = refs.pop(0)
    if not first:
        refs.pop(0)
    rows = capacity + 4 * (capacity // TILE)
    packets = []
    while len(packets) < len(hops):
        group = refs.pop(0)
        for i in range(group.shape[0] // rows):
            packets.append(group.at[i * rows : (i + 1) * rows, :])
    left = refs.pop(0) if last else None
    acc = refs.pop(0)
    if last:
        own, other = refs[:2]
        refs = refs[2:]
    if first:
        acc[...] = jnp.zeros(acc.shape, F32)
    parity = lax.rem(lax.axis_index("blk"), 2)
    offsets = [even if even == odd else jnp.where(parity == 0, even, odd) for even, odd in hops]
    filled = gather_chunks(packets, offsets, capacity, *refs[:5])
    spread(filled, scale, acc, *refs)
    if last:
        balance_step(left, acc, own, other, 0)


def main_call(scale, acc, packets, hops, capacity, left=None):
    first = acc is None
    last = left is not None
    levels = scale.shape[0]
    chunks = capacity // TILE
    slots = len(hops) * chunks + 8
    operands = [scale]
    aliases = {}
    if not first:
        aliases = {1: 0}
        operands.append(acc)
    operands += list(packets)
    out_shape = [jax.ShapeDtypeStruct((levels * G_DEV, TILE), F32)]
    if last:
        operands.append(left)
        half = levels // 2
        out_shape.append(jax.ShapeDtypeStruct((G_DEV // 2, half, TILE), F32))
        out_shape.append(jax.ShapeDtypeStruct((G_DEV // 2, half, TILE), BF16))
    width = JOIN * TILE
    scratch = [pltpu.VMEM(((len(hops) * chunks + 1) * TILE, TILE), BF16)]
    scratch += [pltpu.VMEM((slots, TILE), F32)] * 3
    scratch += [pltpu.SMEM((slots + JOIN,), jnp.int32), pltpu.VMEM((width, TILE), BF16)]
    scratch += [pltpu.VMEM((n, width), F32) for n in (GX, GY, GY, levels)]
    scratch += [pltpu.VMEM((GY, levels, width), F32)] * 2
    return pl.pallas_call(
        functools.partial(main_kernel, hops=hops, capacity=capacity, first=first, last=last),
        out_shape=out_shape,
        in_specs=[VMEM] * len(operands),
        out_specs=[VMEM] * len(out_shape),
        scratch_shapes=scratch,
        input_output_aliases=aliases,
        compiler_params=PARAMS,
    )(*operands)


def finish_kernel(*refs, base):
    own, other = refs[:2]
    out, total, sems = refs[-3:]
    parts = sems.shape[0]
    count = own.shape[0]
    width = count // parts
    copies = []
    for p in range(parts):
        for j in range(p * width, (p + 1) * width):
            total[j] = own[j] + other[j].astype(F32)
        for j in range(p * width, (p + 1) * width):
            copies.append(pltpu.make_async_copy(total.at[j], out.at[:, base + j, :], sems.at[p]))
            copies[-1].start()
    for copy in copies:
        copy.wait()


def finish(own, other, out, base):
    count, half, width = own.shape
    operands = [own, other]
    specs = [VMEM, VMEM]
    aliases = {}
    if out is not None:
        operands.append(out)
        specs.append(pl.BlockSpec(memory_space=pltpu.HBM))
        aliases = {2: 0}
    return pl.pallas_call(
        functools.partial(finish_kernel, base=base),
        out_shape=jax.ShapeDtypeStruct((half, G_DEV, width), F32),
        in_specs=specs,
        out_specs=pl.BlockSpec(memory_space=pltpu.HBM),
        scratch_shapes=[pltpu.VMEM((count, half, width), F32), pltpu.SemaphoreType.DMA((4,))],
        input_output_aliases=aliases,
        compiler_params=PARAMS,
    )(*operands)


def shards(
    obs_weight,
    obs_frac,
    obs_cell,
    obs_level,
    obs_count,
    reach,
    length_x,
    length_y,
    tilt,
    vert_len,
    balance,
):
    levels = balance.shape[0]
    capacity = obs_weight.shape[2]
    blocks = lax.axis_size("blk")
    scales = [v.reshape(1, levels) for v in (length_x, length_y, tilt, vert_len)]
    packet, scale, left = pack(
        obs_count, reach, obs_weight, obs_frac, obs_cell, obs_level, scales, balance
    )

    def move(value, where):
        return lax.ppermute(value, "blk", [(i, where(i) % blocks) for i in range(blocks)])

    def swap(i):
        return i + 1 if i % 2 == 0 else i - 1

    up = move(packet, lambda i: i + 2)
    down = move(packet, lambda i: i - 2)
    near = move(packet, swap)
    cross = move(packet, lambda i: i - 3 if i % 2 == 0 else i + 3)
    (acc,) = main_call(scale, None, (packet,), ((0, 0),), capacity)
    up, down, acc = lax.optimization_barrier((up, down, acc))
    sides = jnp.concatenate([up, down], 0)
    near_sides = move(sides, swap)
    (acc,) = main_call(scale, acc, (sides, near), ((2, 2), (-2, -2), (-1, 1)), capacity)
    cross, acc = lax.optimization_barrier((cross, acc))
    (acc,) = main_call(scale, acc, (cross,), ((3, -3),), capacity)
    near_sides, acc = lax.optimization_barrier((near_sides, acc))
    acc, own, other = main_call(scale, acc, (near_sides,), ((1, 3), (-3, -1)), capacity, left)
    half = levels // 2
    first_other = lax.ppermute(other, "sect", [(0, 1), (1, 0)])
    rest_own, rest_other = pl.pallas_call(
        rest_kernel,
        out_shape=(
            jax.ShapeDtypeStruct((G_DEV // 2, half, TILE), F32),
            jax.ShapeDtypeStruct((G_DEV // 2, half, TILE), BF16),
        ),
        in_specs=[VMEM, VMEM],
        out_specs=(VMEM, VMEM),
        compiler_params=PARAMS,
    )(left, acc)
    second_other = lax.ppermute(rest_other, "sect", [(0, 1), (1, 0)])
    out = finish(own, first_other, None, 0)
    out = finish(rest_own, second_other, out, G_DEV // 2)
    return out


def solution(mesh):
    placed = (
        P(("date", "blk"), "sect", None, None),
        P(("date", "blk"), "sect", None, None),
        P(("date", "blk"), "sect", None),
        P(("date", "blk"), "sect", None),
        P(("date", "blk"), "sect"),
        P(("date", "blk"), None),
        P(),
        P(),
        P(),
        P(),
        P(),
    )
    return jax.shard_map(
        shards,
        mesh=mesh,
        in_specs=placed,
        out_specs=P("sect", ("date", "blk"), None),
        check_vma=False,
    )
```
